32 devices in a mesh: section: 2 (over x), tile: 8 (over z, core), slide: 2 (over y).
Axes of the slice: x: 2, y: 2, z: 4, core: 2. Of those that a mesh axis runs over, the one named last changes fastest.
Arguments:
- features: bfloat16 [2, 16384, 2048], P('slide', ('section', 'tile')), may hold values from -6 to 6
- w_proj: bfloat16 [2048, 1024], P(('section', 'tile', 'slide')), may hold values from -0.25 to 0.25
- w_fc: bfloat16 [1024, 128], replicated, may hold values from -0.1875 to 0.1875
- w_up: bfloat16 [3, 128, 256], replicated, may hold values from -0.5 to 0.5
- w_down: bfloat16 [3, 256, 128], replicated, may hold values from -0.375 to 0.375
- self_adj: bfloat16 [2, 128, 128, 128], P('slide', ('section', 'tile')), may hold values from -0.1875 to 0.1875
- adjacency: bfloat16 [2, 128, 8, 128, 128], P('slide', ('section', 'tile')), may hold values from -0.1875 to 0.1875
- nbr_block: int32 [2, 128, 8], P('slide'), may hold values from 0 to 127, as said below
- counts: int32 [2, 128], P('slide', ('section', 'tile')), may hold values from 6 to 8
Outputs:
- node_out: bfloat16 [2, 16384, 128], P('slide', ('section', 'tile'))
The draws below stay inside these ranges and needn't reach their ends.
Inputs may be any that keep to these rules, and one draw needn't show every extreme that they name: `nbr_block`: block g of a slide is the (g % 8)-th block of the (g // 8)-th group of 8 blocks. Among the 64 entries of one such group, at most 4 name blocks of any one group, and some group is named exactly 4 times; slots beyond counts are named too.
All inputs are finite; a program needn't handle non-finite values.
Results may differ from the reference program's by a relative error of at most 0.015.
Values may be sent and summed in bfloat16 or wider, within the bound.
A program may use at most 64 MiB of HBM per device.

```python
import jax
import jax.numpy as jnp
from jax import lax

F_IN = 2048
F_MID = 1024
H = 128
HID2 = 256
TB = 128
KNB = 8
HOPS = 3
BLK_DEV = 8
SLIDES = 2
NBLK = 128
TILES = 16384


def draw_nbr_block(key, part):
    groups = NBLK // BLK_DEV
    sends = BLK_DEV * KNB
    first, second, third = jax.random.split(key, 3)
    order = jax.vmap(lambda k: jax.random.permutation(k, groups))(jax.random.split(first, SLIDES * groups))
    order = order.reshape(SLIDES, groups, groups)
    shuffle = jax.vmap(lambda k: jax.random.permutation(k, sends))(jax.random.split(second, SLIDES * groups))
    shuffle = shuffle.reshape(SLIDES, groups, sends)
    target = jnp.take_along_axis(order, shuffle % groups, axis=2)
    local = jax.random.randint(third, (SLIDES, groups, sends), 0, BLK_DEV)
    return (target * BLK_DEV + local).reshape(SLIDES, NBLK, KNB).astype(jnp.int32)


def set_ends(result, stream_key, smallest, largest):
    index_at = [jax.random.randint(jax.random.fold_in(stream_key, axis), (), 0, length) for axis, length in enumerate(result.shape)]
    longest = result.shape.index(max(result.shape))
    beside = index_at[:longest] + [(index_at[longest] + 1) % result.shape[longest]] + index_at[longest + 1:]
    return result.at[tuple(index_at)].set(smallest).at[tuple(beside)].set(largest)


def spiked(entries, stream_key, source, target, parts, factor):
    owner, partner = [(jnp.arange(entries.shape[dim]) // (entries.shape[dim] // parts)).reshape([-1 if axis == dim else 1 for axis in range(entries.ndim)]) for dim in (source, target)]
    chosen = jax.random.permutation(stream_key, parts)[partner]
    strong = (owner == chosen) | (owner == (partner + parts // 2) % parts)
    return jnp.where(strong, factor * entries, entries)


def level_of(key, dims, cuts, low, largest):
    gain, own = 1.0, jax.random.fold_in(key, 6)
    for position, shards_of in cuts:
        draws = jnp.exp(jax.random.uniform(jax.random.fold_in(own, position), (shards_of,), jnp.float32, low / len(cuts), largest / len(cuts)))
        gain = gain * jnp.repeat(draws, dims[position] // shards_of).reshape([-1 if axis == position else 1 for axis in range(len(dims))])
    return gain


def centred(own_key, extent, scale, bound, cuts=(), dtype=jnp.bfloat16):
    entries = jax.random.normal(own_key, extent, jnp.float32) * scale
    if len(cuts) > 0:
        entries = level_of(own_key, extent, cuts, -0.22, 0.18) * entries
    return jnp.clip(entries, min=-bound, max=bound).astype(dtype)


def bell_draw_with(stream_key, dims, spread, most, cuts, heavy, held_as=jnp.bfloat16):
    drawn = spread * jax.random.normal(stream_key, dims, jnp.float32)
    if cuts:
        drawn = drawn * level_of(stream_key, dims, cuts, -0.22, 0.18)
    return jnp.clip(spiked(drawn, jax.random.fold_in(stream_key, 3), *heavy), -most, most).astype(held_as)


def setup_inputs(seed: int = 0) -> dict:
    seeds = jax.random.split(jax.random.key(seed), 10)
    return {
        "features": centred(seeds[0], (SLIDES, TILES, F_IN), 1.0, 6.0, ((0, 2), (1, 16))),
        "w_proj": bell_draw_with(seeds[1], (F_IN, F_MID), F_IN ** -0.5, 0.25, ((0, 32),), (0, 1, 32, 2.75)),
        "w_fc": centred(seeds[2], (F_MID, H), F_MID ** -0.5, 0.1875),
        "w_up": centred(seeds[3], (HOPS, H, HID2), H ** -0.5, 0.5),
        "w_down": centred(seeds[4], (HOPS, HID2, H), HID2 ** -0.5, 0.375),
        "self_adj": centred(seeds[5], (SLIDES, NBLK, TB, TB), ((TB * (KNB + 1)) ** -0.5), 0.1875, ((0, 2), (1, 16))),
        "adjacency": centred(seeds[6], (SLIDES, NBLK, KNB, TB, TB), ((TB * (KNB + 1)) ** -0.5), 0.1875, ((0, 2), (1, 16))),
        "nbr_block": draw_nbr_block(jax.random.fold_in(seeds[9], 71), 0),
        "counts": set_ends(jax.random.randint(seeds[8], (SLIDES, NBLK), KNB - 2, KNB + 1), jax.random.fold_in(seeds[8], 1), KNB - 2, KNB).astype(jnp.int32),
    }


def one_slide(features, w_proj, w_fc, w_up, w_down, self_adj, adjacency, nbr_block, counts):
    pre = jnp.dot(features, w_proj, preferred_element_type=jnp.float32)
    encoded = jax.nn.relu(pre).astype(jnp.bfloat16)
    state = jnp.dot(encoded, w_fc, preferred_element_type=jnp.float32)
    live = jnp.arange(KNB).astype(jnp.int32)[None, :] < counts[:, None]
    for hop in range(HOPS):
        nodes = state.astype(jnp.bfloat16).reshape(NBLK, TB, H)
        own = jnp.einsum("bij,bjh->bih", self_adj.astype(jnp.float32), nodes.astype(jnp.float32))

        def push(total, item):
            block_adj, block_nodes, targets, flags = item
            piece = jnp.einsum("kij,jh->kih", block_adj.astype(jnp.float32), block_nodes.astype(jnp.float32))
            piece = jnp.where(flags[:, None, None], piece, 0.0).astype(jnp.bfloat16)
            return total.at[targets.astype(jnp.int32)].add(piece.astype(jnp.float32)), None

        incoming, unused = lax.scan(push, jnp.zeros((NBLK, TB, H), jnp.float32), (adjacency, nodes, nbr_block, live))
        gathered = (own + incoming).astype(jnp.bfloat16).reshape(TILES, H)
        inner = jax.nn.relu(jnp.dot(gathered, w_up[hop], preferred_element_type=jnp.float32)).astype(jnp.bfloat16)
        state = state + jnp.dot(inner, w_down[hop], preferred_element_type=jnp.float32)
    return state.astype(jnp.bfloat16)


def reference(features, w_proj, w_fc, w_up, w_down, self_adj, adjacency, nbr_block, counts):
    results = [one_slide(features[slide_idx], w_proj, w_fc, w_up, w_down, self_adj[slide_idx], adjacency[slide_idx], nbr_block[slide_idx], counts[slide_idx]) for slide_idx in range(SLIDES)]
    return jnp.stack(results)
```

```python
import functools

import jax
import jax.numpy as jnp
from jax import lax
from jax.experimental import pallas as pl
from jax.experimental.pallas import tpu as pltpu
from jax.sharding import PartitionSpec as P

MESH = pl.DeviceIdType.MESH
CORES = 2
PARTS = 4
BF = jnp.bfloat16
F32 = jnp.float32


def remote(src, dst, send_sem, recv_sem, device):
    return pltpu.make_async_remote_copy(
        src_ref=src,
        dst_ref=dst,
        send_sem=send_sem,
        recv_sem=recv_sem,
        device_id=device,
        device_id_type=MESH,
    )


def greet(devices):
    barrier = pltpu.get_barrier_semaphore()
    for device in devices:
        pl.semaphore_signal(barrier, inc=1, device_id=device, device_id_type=MESH)
    return lambda: pl.semaphore_wait(barrier, len(devices))


def whole_kernel(tiles, cap, parts, hops, list_ref, x_hbm, w_ref, fc_hbm, adj_hbm, self_hbm, up_hbm, down_hbm, out_ref, *scratch):
    scratch = list(scratch)

    def take(count):
        taken = scratch[:count]
        del scratch[:count]
        return taken

    x_ref, fc_ref, w_all, acc, adj_ref, self_ref, up_ref, down_ref = take(8)
    pack, adj_e, adj_l, run_e, run_l, state, agg, mine, send1, send2 = take(10)
    nodes_e, nodes_l = take(hops), take(hops)
    recv1, recv2 = take(2)
    ld, z_s, z_r, xy_s, xy_r, dg_s, dg_r, pt_s, pt_r = take(9)
    aj_s, aj_r, nd_s, nd_r, s1, r1, s2, r2 = take(8)

    zs = tiles // CORES
    far = zs // 2
    rows = w_ref.shape[0]
    half = rows // 2
    blocks, tb, width = self_ref.shape[0], self_ref.shape[1], fc_ref.shape[1]
    sends = adj_ref.shape[0] - 1
    kinds = 2 * far
    batch = kinds * cap
    span = 2 * cap
    per = blocks // parts
    sx = lax.axis_index("section")
    sy = lax.axis_index("slide")
    t = lax.axis_index("tile")
    z, c = t // CORES, t % CORES
    ox, oy, oc = 1 - sx, 1 - sy, 1 - c
    oz = z + 1 - 2 * (z % 2)
    partner = {"tile": z * CORES + oc}
    xn, yn = {"section": ox}, {"slide": oy}
    zn, zp = {"tile": oz * CORES + c}, {"tile": oz * CORES + oc}
    places = [z] + [(z + 2 * j) % zs for j in range(1, far)] + [oz] + [(oz + 2 * j) % zs for j in range(1, far)]

    def zdev(j):
        return {"tile": ((z + 2 * j) % zs) * CORES + c}

    started = []

    def go(src, dst, ss, rs, device, log=started):
        copy = remote(src, dst, ss, rs, device)
        copy.start()
        log.append(copy)

    def arrived(dst, ss, rs, device):
        remote(dst, dst, ss, rs, device).wait_recv()

    loads = [
        pltpu.make_async_copy(src, dst, ld.at[i])
        for i, (src, dst) in enumerate(
            (
                (adj_hbm, adj_ref.at[pl.ds(0, sends)]),
                (x_hbm, x_ref),
                (fc_hbm, fc_ref),
                (self_hbm, self_ref),
                (up_hbm, up_ref),
                (down_hbm, down_ref),
            )
        )
    ]
    wait = greet([partner, xn, yn, zn, zp] + [zdev(j) for j in range(1, far)])
    for load in loads:
        load.start()
    start = ((sx * tiles + t) * 2 + sy) * rows
    w_all[pl.ds(pl.multiple_of(start, rows), rows)] = w_ref[...]
    adj_ref[sends] = jnp.zeros((tb, tb), BF)
    run_e[kinds * span] = jnp.zeros((tb, width), F32)
    run_l[kinds * span] = jnp.zeros((tb, width), F32)
    wait()

    def own(k):
        return w_ref.at[pl.ds(k * half, half)]

    def at(x, m, core, y, k):
        first = ((x * tiles + places[m] * CORES + core) * 2 + y) * rows + k * half
        return w_all.at[pl.ds(pl.multiple_of(first, half), half)]

    for k in range(2):
        for j in range(1, far):
            go(own(k), at(sx, 0, c, sy, k), z_s.at[j, k], z_r.at[j, k], zdev(j))
    for k in range(2):
        go(own(k), at(sx, 0, c, sy, k), z_s.at[far, k], z_r.at[far, k], zn)

    def line(m, k):
        here = at(sx, m, c, sy, k)
        src = here if m else own(k)
        if 0 < m < far:
            arrived(here, z_s.at[0, k], z_r.at[far - m, k], zdev(m))
        elif m:
            arrived(here, z_s.at[0, k], z_r.at[m, k], zn)
        go(src, here, xy_s.at[0, m, k], xy_r.at[0, m, k], xn)
        go(src, here, xy_s.at[1, m, k], xy_r.at[1, m, k], yn)
        if 0 < m < far:
            go(src, here, z_s.at[far + m, k], z_r.at[far + m, k], zn)
        go(src, here, pt_s.at[0, m, k], pt_r.at[0, m, k], partner)

    def cross(m, k):
        for kind, device, other, ref in (
            (0, xn, yn, at(ox, m, c, sy, k)),
            (1, yn, xn, at(sx, m, c, oy, k)),
        ):
            arrived(ref, xy_s.at[kind, m, k], xy_r.at[kind, m, k], device)
            if k == kind:
                go(ref, ref, dg_s.at[m, k], dg_r.at[m, k], other)
            go(ref, ref, pt_s.at[1 + kind, m, k], pt_r.at[1 + kind, m, k], partner)

    def corner(m, k):
        ref = at(ox, m, c, oy, k)
        arrived(ref, dg_s.at[m, k], dg_r.at[m, k], (yn, xn)[k])
        go(ref, ref, pt_s.at[3, m, k], pt_r.at[3, m, k], partner)

    def pack_tiles():
        def keep(i, carry):
            adj_e[i] = adj_ref[list_ref[i]]
            return carry

        def other(i, carry):
            pack[i] = adj_ref[list_ref[batch + i]]
            return carry

        lax.fori_loop(0, batch, keep, 0, unroll=4)
        lax.fori_loop(0, 3 * batch, other, 0, unroll=4)
        go(pack.at[pl.ds(0, batch)], adj_e.at[pl.ds(batch, batch)], aj_s.at[0, 0], aj_r.at[0, 0], partner)

    bit = batch // 2

    def send_tiles():
        for piece in range(2):
            for m, device in ((1, zn), (2, zp)):
                go(
                    pack.at[pl.ds(m * batch + piece * bit, bit)],
                    adj_l.at[pl.ds((m - 1) * batch + piece * bit, bit)],
                    aj_s.at[m, piece],
                    aj_r.at[m, piece],
                    device,
                )

    def nodes_out(hop, p):
        first = p * per
        here = nodes_e[hop].at[pl.ds(first, per)]
        go(here, nodes_e[hop].at[pl.ds(blocks + first, per)], nd_s.at[hop, 0, p], nd_r.at[hop, 0, p], partner)
        go(here, nodes_l[hop].at[pl.ds(first, per)], nd_s.at[hop, 1, p], nd_r.at[hop, 1, p], zn)

    depth = CORES * 2 * rows
    tall = per * tb

    def multiply(m):
        for k in range(2):
            for kind, (x, y) in enumerate(((sx, sy), (ox, sy), (sx, oy), (ox, oy))):
                arrived(at(x, m, oc, y, k), pt_s.at[kind, m, k], pt_r.at[kind, m, k], partner)
        slabs = [pl.ds(pl.multiple_of((x * zs + places[m]) * depth, depth), depth) for x in (sx, ox)]

        def product(strip):
            total = jnp.dot(x_ref[strip, slabs[0]], w_all[slabs[0], :], preferred_element_type=F32)
            return total + jnp.dot(x_ref[strip, slabs[1]], w_all[slabs[1], :], preferred_element_type=F32)

        if m < zs - 1:

            def body(i, carry):
                strip = pl.ds(pl.multiple_of(i * tall, tall), tall)
                total = product(strip)
                acc[strip, :] = total + acc[strip, :] if m else total
                return carry

            lax.fori_loop(0, parts, body, 0)
            return
        for p in range(parts):
            strip = pl.ds(p * tall, tall)
            enc = jnp.maximum(product(strip) + acc[strip, :], 0.0).astype(BF)
            first = jnp.dot(enc, fc_ref[...], preferred_element_type=F32)
            state[strip, :] = first
            nodes_e[0][pl.ds(p * per, per)] = first.astype(BF).reshape(per, tb, width)
            nodes_out(0, p)

    steps = [(m, k) for m in range(zs) for k in range(2)]
    count = len(steps)
    for step in range(count + 5):
        if step < count:
            line(*steps[step])
        if step == 1:
            loads[0].wait()
            pack_tiles()
        if step == 2 * far:
            send_tiles()
        if 0 <= step - 2 < count:
            cross(*steps[step - 2])
        if 0 <= step - 4 < count:
            corner(*steps[step - 4])
        if step == 5:
            for load in loads[1:]:
                load.wait()
        if 0 <= step - 5 < count and steps[step - 5][1]:
            multiply(steps[step - 5][0])

    at_a, at_n, at_k, at_l = (4 * batch + i * 2 * kinds * span for i in range(4))

    def runs(phase, k, hop):
        tiles_ref, nodes_ref, run = ((adj_e, nodes_e[hop], run_e), (adj_l, nodes_l[hop], run_l))[phase]
        total = None
        for i in range(span):
            e = (phase * kinds + k) * span + i
            one = jnp.dot(tiles_ref[list_ref[at_a + e]], nodes_ref[list_ref[at_n + e]], preferred_element_type=F32)
            total = one if total is None else total * list_ref[at_k + e].astype(F32) + one
            run[k * span + i] = total

    def block_sum(k, r):
        return run_e[list_ref[at_l + k * blocks + r]] + run_l[list_ref[at_l + (kinds + k) * blocks + r]]

    waiting = []
    for hop in range(hops):
        def own_block(b, carry):
            agg[b] = jnp.dot(self_ref[b], nodes_e[hop][b], preferred_element_type=F32)
            return carry

        lax.fori_loop(0, blocks, own_block, 0, unroll=2)
        for p in range(parts):
            ref = nodes_e[hop].at[pl.ds(blocks + p * per, per)]
            arrived(ref, nd_s.at[hop, 0, p], nd_r.at[hop, 0, p], partner)
        if hop == 0:
            ref = adj_e.at[pl.ds(batch, batch)]
            arrived(ref, aj_s.at[0, 0], aj_r.at[0, 0], partner)

        def early(k, carry):
            runs(0, k, hop)
            return carry

        lax.fori_loop(0, kinds, early, 0)
        for p in range(parts):
            ref = nodes_l[hop].at[pl.ds(p * per, per)]
            arrived(ref, nd_s.at[hop, 1, p], nd_r.at[hop, 1, p], zn)
            go(ref, nodes_l[hop].at[pl.ds(blocks + p * per, per)], nd_s.at[hop, 2, p], nd_r.at[hop, 2, p], partner)
        if hop == 0:
            for piece in range(2):
                for m, device in ((1, zn), (2, zp)):
                    ref = adj_l.at[pl.ds((m - 1) * batch + piece * bit, bit)]
                    arrived(ref, aj_s.at[m, piece], aj_r.at[m, piece], device)
        for p in range(parts):
            ref = nodes_l[hop].at[pl.ds(blocks + p * per, per)]
            arrived(ref, nd_s.at[hop, 2, p], nd_r.at[hop, 2, p], partner)

        for copy in waiting:
            copy.wait_send()
        waiting = []

        def across(j, k):
            runs(1, k, hop)
            for p in range(parts):
                for r in range(p * per, p * per + per):
                    send1[j, r] = block_sum(k, r).astype(BF)
                piece = pl.ds(p * per, per)
                go(send1.at[j, piece], recv1.at[hop, j, piece], s1.at[hop, j, p], r1.at[hop, j, p], xn, waiting)

        def crossed(j, p):
            ref = recv1.at[hop, j, pl.ds(p * per, per)]
            arrived(ref, s1.at[hop, j, p], r1.at[hop, j, p], xn)

        for j in range(1, far):
            across(j, 2 * j)
        for j in range(1, far):
            runs(1, 2 * j + 1, hop)
            for r in range(blocks):
                mine[j - 1, r] = block_sum(2 * j + 1, r)
        across(0, 0)
        runs(1, 1, hop)
        for r in range(blocks):
            agg[r] += block_sum(1, r)
        for p in range(parts):
            piece = pl.ds(p * per, per)
            for j in range(1, far):
                crossed(j, p)
                send2[j - 1, piece] = (mine[j - 1, piece] + recv1[hop, j, piece].astype(F32)).astype(BF)
                go(send2.at[j - 1, piece], recv2.at[hop, j - 1, piece], s2.at[hop, j - 1, p], r2.at[hop, j - 1, p], zdev(j), waiting)
        for p in range(parts):
            piece = pl.ds(p * per, per)
            strip = pl.ds(p * tall, tall)
            crossed(0, p)
            total = agg[piece] + recv1[hop, 0, piece].astype(F32)
            for j in range(1, far):
                arrived(recv2.at[hop, j - 1, piece], s2.at[hop, j - 1, p], r2.at[hop, j - 1, p], zdev(j))
                total += recv2[hop, j - 1, piece].astype(F32)
            gathered = total.astype(BF).reshape(tall, width)
            inner = jnp.dot(gathered, up_ref[hop], preferred_element_type=F32)
            inner = jnp.maximum(inner, 0.0).astype(BF)
            after = state[strip, :] + jnp.dot(inner, down_ref[hop], preferred_element_type=F32)
            if hop == hops - 1:
                out_ref[strip, :] = after.astype(BF)
            else:
                state[strip, :] = after
                nodes_e[hop + 1][piece] = after.astype(BF).reshape(per, tb, width)
                nodes_out(hop + 1, p)
    for copy in started + waiting:
        copy.wait_send()


def fused(rows, w_proj, w_fc, w_up, w_down, self_adj, adjacency, lists, cap):
    tiles = lax.axis_size("tile")
    zs = tiles // CORES
    far = zs // 2
    blocks, slots, tb, _ = adjacency.shape
    width = w_fc.shape[1]
    hops = w_up.shape[0]
    parts = PARTS if blocks % PARTS == 0 else 1
    kinds = 2 * far
    batch = kinds * cap
    span = 2 * cap
    distant = max(1, far - 1)
    vmem = pl.BlockSpec(memory_space=pltpu.VMEM)
    hbm = pl.BlockSpec(memory_space=pltpu.HBM)
    dma = pltpu.SemaphoreType.DMA
    tile = (tb, tb)
    piece = (blocks, tb, width)
    return pl.pallas_call(
        functools.partial(whole_kernel, tiles, cap, parts, hops),
        out_shape=jax.ShapeDtypeStruct((rows.shape[0], width), BF),
        in_specs=[pl.BlockSpec(memory_space=pltpu.SMEM), hbm, vmem] + [hbm] * 5,
        out_specs=vmem,
        scratch_shapes=[
            pltpu.VMEM(rows.shape, BF),
            pltpu.VMEM(w_fc.shape, BF),
            pltpu.VMEM((rows.shape[1], w_proj.shape[1]), BF),
            pltpu.VMEM((rows.shape[0], w_proj.shape[1]), F32),
            pltpu.VMEM((blocks * slots + 1,) + tile, BF),
            pltpu.VMEM(self_adj.shape, BF),
            pltpu.VMEM(w_up.shape, BF),
            pltpu.VMEM(w_down.shape, BF),
            pltpu.VMEM((3 * batch,) + tile, BF),
            pltpu.VMEM((2 * batch,) + tile, BF),
            pltpu.VMEM((2 * batch,) + tile, BF),
            pltpu.VMEM((kinds * span + 1, tb, width), F32),
            pltpu.VMEM((kinds * span + 1, tb, width), F32),
            pltpu.VMEM((rows.shape[0], width), F32),
            pltpu.VMEM(piece, F32),
            pltpu.VMEM((distant,) + piece, F32),
            pltpu.VMEM((far,) + piece, BF),
            pltpu.VMEM((distant,) + piece, BF),
        ]
        + [pltpu.VMEM((2 * blocks, tb, width), BF)] * (2 * hops)
        + [pltpu.VMEM((hops, far) + piece, BF), pltpu.VMEM((hops, distant) + piece, BF)]
        + [dma((6,))]
        + [dma((zs, 2))] * 2
        + [dma((2, zs, 2))] * 2
        + [dma((zs, 2))] * 2
        + [dma((4, zs, 2))] * 2
        + [dma((3, 2))] * 2
        + [dma((hops, 3, parts))] * 2
        + [dma((hops, far, parts))] * 2
        + [dma((hops, distant, parts))] * 2,
        compiler_params=pltpu.CompilerParams(
            collective_id=0, has_side_effects=True, vmem_limit_bytes=62 << 20
        ),
        name="whole",
    )(lists, rows, w_proj, w_fc, adjacency.reshape((blocks * slots,) + tile), self_adj, w_up, w_down)


def tile_lists(neighbours, counts, slots, cap):
    tiles = lax.axis_size("tile")
    zs = tiles // CORES
    far = zs // 2
    kinds = 2 * far
    span = 2 * cap
    blocks = counts.shape[0]
    sends = blocks * slots
    x = lax.axis_index("section")
    t = lax.axis_index("tile")
    z, c = t // CORES, t % CORES
    oz = z + 1 - 2 * (z % 2)
    seats = [(z, c), (z, 1 - c), (oz, c), (oz, 1 - c)]
    entries = neighbours.reshape(-1)

    def group(gx, gz, gc):
        return gx * tiles + gz * CORES + gc

    def receivers(seat):
        gz, gc = seat
        return [group(gx, (gz + 2 * j) % zs, gc) for j in range(far) for gx in (1 - x, x)]

    named = jnp.stack(
        [lax.dynamic_slice_in_dim(entries, group(x, gz, gc) * sends, sends) for gz, gc in seats]
    )
    place = jnp.arange(sends, dtype=jnp.int32)
    key = named * sends + place
    rank = jnp.sum((key[:, None, :] < key[:, :, None]).astype(jnp.int32), axis=2)
    live = (jnp.arange(slots, dtype=jnp.int32)[None, :] < counts[:, None]).reshape(sends)
    wanted = jnp.stack([g for seat in seats for g in receivers(seat)])
    wanted = (wanted[:, None] * cap + jnp.arange(cap, dtype=jnp.int32)[None, :]).reshape(-1)
    hit = (wanted[:, None] == rank[0][None, :]) & live[None, :]
    packed = sends + jnp.sum(jnp.where(hit, place[None, :] - sends, 0), axis=1)

    both = named.reshape(2, 2 * sends)
    seat_of = jnp.arange(2 * sends, dtype=jnp.int32) // sends
    key = both * (2 * sends) + jnp.arange(2 * sends, dtype=jnp.int32)
    order = jnp.sum((key[:, None, :] < key[:, :, None]).astype(jnp.int32), axis=2)
    tile_at = seat_of * (kinds * cap) + rank.reshape(2, 2 * sends) - (both // blocks) * cap
    node_at = jnp.arange(2 * sends, dtype=jnp.int32) // slots
    code = ((tile_at * (2 * blocks)) + node_at) * blocks + both % blocks
    mine = jnp.stack(receivers(seats[0]))
    ask = (mine[:, None] * span + jnp.arange(span, dtype=jnp.int32)[None, :]).reshape(-1)
    hit = ask[None, :, None] == order[:, None, :]
    code = jnp.sum(jnp.where(hit, code[:, None, :], 0), axis=2).reshape(2, kinds, span)
    block = code % blocks
    node = (code // blocks) % (2 * blocks)
    kind = jnp.arange(kinds, dtype=jnp.int32)[None, :, None]
    tile = code // (2 * blocks * blocks) + kind * cap
    first = jnp.arange(span, dtype=jnp.int32)[None, None, :] > 0
    same = first & (block == jnp.roll(block, 1, axis=2))
    want = jnp.arange(blocks, dtype=jnp.int32)[None, None, :, None]
    upto = jnp.sum((block[:, :, None, :] <= want).astype(jnp.int32), axis=3)
    there = jnp.any(block[:, :, None, :] == want, axis=3)
    last = jnp.where(there, kind * span + upto - 1, kinds * span)
    return jnp.concatenate(
        [packed, tile.reshape(-1), node.reshape(-1), same.astype(jnp.int32).reshape(-1), last.reshape(-1)]
    )


def local(features, w_proj, w_fc, w_up, w_down, self_adj, adjacency, nbr_block, counts):
    rows = features[0]
    blocks = self_adj.shape[1]
    tb = self_adj.shape[2]
    width = w_fc.shape[1]
    slots = adjacency.shape[2]
    hops = w_up.shape[0]
    peers = lax.axis_size("section") * lax.axis_size("tile")
    me_index = lax.axis_index("section") * lax.axis_size("tile") + lax.axis_index("tile")
    sends = blocks * slots
    cap = (sends + peers - 1) // peers
    live = jnp.arange(slots, dtype=jnp.int32)[None, :] < counts[0][:, None]
    square = lax.axis_size("section") == 2 and lax.axis_size("slide") == 2
    pairs = lax.axis_size("tile") % (2 * CORES) == 0
    if square and pairs and sends == peers * cap and w_proj.shape[0] % 32 == 0:
        lists = tile_lists(nbr_block[0], counts[0], slots, cap)
        return fused(rows, w_proj, w_fc, w_up, w_down, self_adj[0], adjacency[0], lists, cap)[None]
    pre = jnp.dot(
        rows,
        lax.all_gather(w_proj, ("section", "tile", "slide"), axis=0, tiled=True),
        preferred_element_type=F32,
    )
    encoded = jax.nn.relu(pre).astype(BF)
    state = jnp.dot(encoded, w_fc, preferred_element_type=F32)
    table = nbr_block[0].reshape(peers, sends)
    target_dev = table // blocks
    target_local = table % blocks
    positions = jnp.arange(sends, dtype=jnp.int32)
    before = positions[None, :] < positions[:, None]
    same = target_dev[:, :, None] == target_dev[:, None, :]
    ranking = jnp.sum(jnp.logical_and(same, before[None]).astype(jnp.int32), axis=2)
    mine_dev = lax.dynamic_index_in_dim(target_dev, me_index, 0, keepdims=False)
    mine_rank = lax.dynamic_index_in_dim(ranking, me_index, 0, keepdims=False)
    slot_of = mine_dev * cap + mine_rank
    send_map = (jnp.arange(peers * cap, dtype=jnp.int32)[:, None] == slot_of[None, :]).astype(BF)
    arrive_hit = target_dev == me_index
    slot_flags = jnp.logical_and(
        arrive_hit[:, :, None],
        ranking[:, :, None] == jnp.arange(cap, dtype=jnp.int32)[None, None, :],
    ).astype(F32)
    local_flags = (
        target_local[:, :, None] == jnp.arange(blocks, dtype=jnp.int32)[None, None, :]
    ).astype(F32)
    recv_map = (
        jnp.einsum("pjc,pjr->rpc", slot_flags, local_flags).reshape(blocks, peers * cap).astype(BF)
    )
    for hop in range(hops):
        nodes = state.astype(BF).reshape(blocks, tb, width)
        own = jnp.einsum("bij,bjh->bih", self_adj[0], nodes, preferred_element_type=F32)
        terms = jnp.einsum("bkij,bjh->bkih", adjacency[0], nodes, preferred_element_type=F32)
        terms = (
            jnp.where(live[:, :, None, None], terms, 0.0).astype(BF).reshape(sends, tb * width)
        )
        outgoing = jnp.dot(send_map, terms, preferred_element_type=F32).astype(BF)
        outgoing = outgoing.reshape(peers, cap, tb, width)
        arrived = lax.all_to_all(
            outgoing, ("section", "tile"), split_axis=0, concat_axis=0, tiled=True
        )
        arrived = arrived.reshape(peers * cap, tb * width)
        incoming = jnp.dot(recv_map, arrived, preferred_element_type=F32).reshape(
            blocks, tb, width
        )
        gathered = (own + incoming).astype(BF).reshape(blocks * tb, width)
        inner = jax.nn.relu(jnp.dot(gathered, w_up[hop], preferred_element_type=F32)).astype(BF)
        state = state + jnp.dot(inner, w_down[hop], preferred_element_type=F32)
    return state.astype(BF)[None]


def solution(mesh):
    return jax.shard_map(
        local,
        mesh=mesh,
        in_specs=(
            P("slide", ("section", "tile"), None),
            P(("section", "tile", "slide"), None),
            P(),
            P(),
            P(),
            P("slide", ("section", "tile"), None, None),
            P("slide", ("section", "tile"), None, None, None),
            P("slide", None, None),
            P("slide", ("section", "tile")),
        ),
        out_specs=P("slide", ("section", "tile"), None),
        check_vma=False,
    )
```

```python
import functools

import jax
import jax.numpy as jnp
from jax import lax
from jax.experimental import pallas as pl
from jax.experimental.pallas import tpu as pltpu
from jax.sharding import PartitionSpec as P

MESH = pl.DeviceIdType.MESH
CORES = 2
LANES = 128
PARTS = 4
BF = jnp.bfloat16
F32 = jnp.float32


def remote(src, dst, send_sem, recv_sem, device):
    return pltpu.make_async_remote_copy(
        src_ref=src,
        dst_ref=dst,
        send_sem=send_sem,
        recv_sem=recv_sem,
        device_id=device,
        device_id_type=MESH,
    )


def greet(devices):
    barrier = pltpu.get_barrier_semaphore()
    for device in devices:
        pl.semaphore_signal(barrier, inc=1, device_id=device, device_id_type=MESH)
    return lambda: pl.semaphore_wait(barrier, len(devices))


def make_lists(named_ref, counts_ref, table, chips, sizes, place):
    tiles, cap, blocks, far = sizes
    sx, z, oz, c = place
    zs = tiles // CORES
    kinds = 2 * far
    span = 2 * cap
    both = CORES * blocks
    slots = named_ref.shape[0]
    sends = blocks * slots

    def iota(shape, axis):
        return lax.broadcasted_iota(jnp.int32, shape, axis)

    def receiver(kind, gz, gc):
        gx = jnp.where(kind % 2 == 0, 1 - sx, sx)
        return gx * tiles + (gz + 2 * (kind // 2)) % zs * CORES + gc

    lane = iota((1, LANES), 1)
    wide = (LANES, LANES)
    entry = iota(wide, 0)
    column = iota(wide, 1)
    same_core = (entry // blocks) % CORES == (column // blocks) % CORES
    limit = jnp.zeros((1, LANES), jnp.int32)
    for b in range(blocks):
        limit = jnp.where(lane % blocks == b, counts_ref[b], limit)
    alive = (lane // both < limit) & ((lane // blocks) % CORES == c)
    alive = jnp.where(alive, (lane % blocks) * slots + lane // both - sends, 0)
    alive = jnp.transpose(jnp.broadcast_to(alive, wide))
    for phase in range(2):
        row = jnp.zeros((1, LANES), jnp.int32)
        for slot in range(slots):
            moved = pltpu.roll(named_ref[pl.ds(slot, 1), :], (slot * both - chips[phase] * both + LANES) % LANES, 1)
            row = jnp.where(lane // both == slot, moved, row)
        across = jnp.broadcast_to(row * LANES + lane, wide)
        down = jnp.transpose(across)
        named = down // LANES
        less = across < down
        order = jnp.sum(jnp.where(less, 1, 0), axis=1, keepdims=True)
        rank = jnp.sum(jnp.where(less & same_core, 1, 0), axis=1, keepdims=True)
        if phase == 0:
            person = column // (kinds * cap)
            kind = (column // cap) % kinds
            core = jnp.where(person % 2 == 0, c, 1 - c)
            want = receiver(kind, jnp.where(person < 2, z, oz), core) * cap + column % cap
            packed = jnp.sum(jnp.where(rank == want, alive, 0), axis=0, keepdims=True)
            table[pl.ds(0, 1), :] = packed + sends
        kind = column // span % kinds
        want = receiver(kind, z, c) * span + column % span
        hit = order == want
        core = (entry // blocks) % CORES
        rank = jnp.clip(rank - named // blocks * cap, 0, cap - 1)
        if phase == 0:
            tile = core * (kinds * cap) + kind * cap + rank
        else:
            tile = jnp.where(kind < 2, core, core * (kinds - 2) + kind - 2) * cap + rank

        def chosen(value):
            return jnp.sum(jnp.where(hit, value, 0), axis=0, keepdims=True)

        block = chosen(named % blocks)
        table[pl.ds(1 + phase, 1), :] = chosen(tile)
        table[pl.ds(3 + phase, 1), :] = chosen(entry % both)
        again = (lane % span > 0) & (block == pltpu.roll(block, 1, 1))
        table[pl.ds(5 + phase, 1), :] = jnp.where(again, 1, 0)
        block = jnp.transpose(jnp.broadcast_to(block, wide))
        fits = (entry // span == column // blocks) & (entry < kinds * span)
        upto = jnp.sum(jnp.where(fits & (block <= column % blocks), 1, 0), axis=0, keepdims=True)
        there = jnp.sum(jnp.where(fits & (block == column % blocks), 1, 0), axis=0, keepdims=True)
        last = lane // blocks * span + upto - 1
        table[pl.ds(7 + phase, 1), :] = jnp.where(there > 0, last, kinds * span)


def whole_kernel(tiles, cap, parts, hops, counts_hbm, named_hbm, x_hbm, w_hbm, fc_hbm, adj_hbm, self_hbm, up_hbm, down_hbm, out_ref, *scratch):
    scratch = list(scratch)

    def take(count):
        taken = scratch[:count]
        del scratch[:count]
        return taken

    x_ref, fc_ref, w_all, acc, adj_ref, self_ref, up_ref, down_ref = take(8)
    table, lists, named_ref, counts_ref = take(4)
    pack, adj_e, adj_x, adj_n, adj_f, run_e, run_l, state, agg, mine, send1, send2 = take(12)
    nodes_e, nodes_l = take(hops), take(hops)
    recv1, recv2 = take(2)
    ld, z_s, z_r, xy_s, xy_r, dg_s, dg_r, pt_s, pt_r = take(9)
    aj_s, aj_r, nd_s, nd_r, s1, r1, s2, r2 = take(8)

    zs = tiles // CORES
    far = zs // 2
    rows = w_hbm.shape[0]
    half = rows // 2
    blocks, tb, width = self_ref.shape[0], self_ref.shape[1], fc_ref.shape[1]
    sends = adj_ref.shape[0] - 1
    kinds = 2 * far
    batch = kinds * cap
    span = 2 * cap
    per = blocks // parts
    sx = lax.axis_index("section")
    sy = lax.axis_index("slide")
    t = lax.axis_index("tile")
    z, c = t // CORES, t % CORES
    ox, oy, oc = 1 - sx, 1 - sy, 1 - c
    oz = z + 1 - 2 * (z % 2)
    partner = {"tile": z * CORES + oc}
    xn, yn = {"section": ox}, {"slide": oy}
    zn, zp = {"tile": oz * CORES + c}, {"tile": oz * CORES + oc}
    places = [z] + [(z + 2 * j) % zs for j in range(1, far)] + [oz] + [(oz + 2 * j) % zs for j in range(1, far)]

    def zdev(j):
        return {"tile": ((z + 2 * j) % zs) * CORES + c}

    started = []

    def go(src, dst, ss, rs, device, log=started):
        copy = remote(src, dst, ss, rs, device)
        copy.start()
        log.append(copy)

    def arrived(dst, ss, rs, device):
        remote(dst, dst, ss, rs, device).wait_recv()

    start = ((sx * tiles + t) * 2 + sy) * rows
    loads = [
        pltpu.make_async_copy(src, dst, ld.at[i])
        for i, (src, dst) in enumerate(
            (
                (w_hbm, w_all.at[pl.ds(pl.multiple_of(start, rows), rows)]),
                (adj_hbm, adj_ref.at[pl.ds(0, sends)]),
                (x_hbm, x_ref),
                (fc_hbm, fc_ref),
                (self_hbm, self_ref),
                (up_hbm, up_ref),
                (down_hbm, down_ref),
                (named_hbm, named_ref),
                (counts_hbm, counts_ref),
            )
        )
    ]
    wait = greet([partner, xn, yn, zn, zp] + [zdev(j) for j in range(1, far)])
    for load in loads:
        load.start()
    adj_ref[sends] = jnp.zeros((tb, tb), BF)
    run_e[kinds * span] = jnp.zeros((tb, width), F32)
    run_l[kinds * span] = jnp.zeros((tb, width), F32)

    loads[0].wait()
    wait()

    def at(x, m, core, y, k):
        first = ((x * tiles + places[m] * CORES + core) * 2 + y) * rows + k * half
        return w_all.at[pl.ds(pl.multiple_of(first, half), half)]

    for k in range(2):
        for j in range(1, far):
            go(at(sx, 0, c, sy, k), at(sx, 0, c, sy, k), z_s.at[j, k], z_r.at[j, k], zdev(j))
    for k in range(2):
        go(at(sx, 0, c, sy, k), at(sx, 0, c, sy, k), z_s.at[far, k], z_r.at[far, k], zn)

    def line(m, k):
        here = at(sx, m, c, sy, k)
        if 0 < m < far:
            arrived(here, z_s.at[0, k], z_r.at[far - m, k], zdev(m))
        elif m:
            arrived(here, z_s.at[0, k], z_r.at[m, k], zn)
        go(here, here, xy_s.at[0, m, k], xy_r.at[0, m, k], xn)
        go(here, here, xy_s.at[1, m, k], xy_r.at[1, m, k], yn)
        if 0 < m < far:
            go(here, here, z_s.at[far + m, k], z_r.at[far + m, k], zn)
        go(here, here, pt_s.at[0, m, k], pt_r.at[0, m, k], partner)

    def cross(m, k):
        for kind, device, other, ref in (
            (0, xn, yn, at(ox, m, c, sy, k)),
            (1, yn, xn, at(sx, m, c, oy, k)),
        ):
            arrived(ref, xy_s.at[kind, m, k], xy_r.at[kind, m, k], device)
            if k == kind:
                go(ref, ref, dg_s.at[m, k], dg_r.at[m, k], other)
            go(ref, ref, pt_s.at[1 + kind, m, k], pt_r.at[1 + kind, m, k], partner)

    def corner(m, k):
        ref = at(ox, m, c, oy, k)
        arrived(ref, dg_s.at[m, k], dg_r.at[m, k], (yn, xn)[k])
        go(ref, ref, pt_s.at[3, m, k], pt_r.at[3, m, k], partner)

    def pack_tiles():
        def keep(i, carry):
            adj_e[c * batch + i] = adj_ref[lists[0, i]]
            return carry

        def other(i, carry):
            pack[i] = adj_ref[lists[0, batch + i]]
            return carry

        lax.fori_loop(0, batch, keep, 0, unroll=4)
        lax.fori_loop(0, 3 * batch, other, 0, unroll=4)
        theirs = adj_e.at[pl.ds(pl.multiple_of(c * batch, batch), batch)]
        go(pack.at[pl.ds(0, batch)], theirs, aj_s.at[0, 0], aj_r.at[0, 0], partner)

    near = 2 * cap
    stretch = ((adj_x, 0, cap), (adj_n, cap, cap), (adj_f, near, batch - near))

    def send_tiles(piece):
        into, first, size = stretch[piece]
        for m, device in ((1, zn), (2, zp)):
            there = into.at[pl.ds(pl.multiple_of(c * size, size), size)]
            go(pack.at[pl.ds(m * batch + first, size)], there, aj_s.at[m, piece], aj_r.at[m, piece], device)

    def tiles_in(piece):
        into, first, size = stretch[piece]
        for m, device, core in ((1, zn, c), (2, zp, oc)):
            ref = into.at[pl.ds(pl.multiple_of(core * size, size), size)]
            arrived(ref, aj_s.at[m, piece], aj_r.at[m, piece], device)

    def seat(core, p):
        return pl.ds(pl.multiple_of(core * blocks + p * per, per), per)

    def nodes_out(hop, p, after):
        here = nodes_e[hop].at[seat(c, p)]
        here[...] = after.astype(BF).reshape(per, tb, width)
        go(here, here, nd_s.at[hop, 0, p], nd_r.at[hop, 0, p], partner)
        go(here, nodes_l[hop].at[seat(c, p)], nd_s.at[hop, 1, p], nd_r.at[hop, 1, p], zn)

    depth = CORES * 2 * rows
    tall = per * tb

    def multiply(m):
        for k in range(2):
            for kind, (x, y) in enumerate(((sx, sy), (ox, sy), (sx, oy), (ox, oy))):
                arrived(at(x, m, oc, y, k), pt_s.at[kind, m, k], pt_r.at[kind, m, k], partner)
        slabs = [pl.ds(pl.multiple_of((x * zs + places[m]) * depth, depth), depth) for x in (sx, ox)]

        def product(strip):
            total = jnp.dot(x_ref[strip, slabs[0]], w_all[slabs[0], :], preferred_element_type=F32)
            return total + jnp.dot(x_ref[strip, slabs[1]], w_all[slabs[1], :], preferred_element_type=F32)

        if m < zs - 1:

            def body(i, carry):
                strip = pl.ds(pl.multiple_of(i * tall, tall), tall)
                total = product(strip)
                acc[strip, :] = total + acc[strip, :] if m else total
                return carry

            lax.fori_loop(0, parts, body, 0)
            return
        for p in range(parts):
            strip = pl.ds(p * tall, tall)
            enc = jnp.maximum(product(strip) + acc[strip, :], 0.0).astype(BF)
            first = jnp.dot(enc, fc_ref[...], preferred_element_type=F32)
            state[strip, :] = first
            nodes_out(0, p, first)
        send_tiles(1)

    steps = [(m, k) for m in range(zs) for k in range(2)]
    count = len(steps)
    for step in range(count + 5):
        if step < count:
            line(*steps[step])
        if step == 1:
            for load in loads[7:]:
                load.wait()
            make_lists(named_ref, counts_ref, table, [sx * zs + z, sx * zs + oz], (tiles, cap, blocks, far), (sx, z, oz, c))
            spread = pltpu.make_async_copy(table, lists, ld.at[9])
            spread.start()
            loads[1].wait()
            spread.wait()
            pack_tiles()
        if step == 2 * far - 1:
            send_tiles(2)
            send_tiles(0)
        if 0 <= step - 2 < count:
            cross(*steps[step - 2])
        if 0 <= step - 4 < count:
            corner(*steps[step - 4])
        if step == 5:
            for load in loads[2:7]:
                load.wait()
        if 0 <= step - 5 < count and steps[step - 5][1]:
            multiply(steps[step - 5][0])

    def runs(phase, k, hop):
        nodes_ref, run = ((nodes_e[hop], run_e), (nodes_l[hop], run_l))[phase]
        tiles_ref = adj_e if phase == 0 else (adj_x, adj_n, adj_f)[min(k, 2)]
        total = None
        for i in range(span):
            e = k * span + i
            tile, node = lists[1 + phase, e], lists[3 + phase, e]
            one = jnp.dot(tiles_ref[tile], nodes_ref[node], preferred_element_type=F32)
            total = one if total is None else total * lists[5 + phase, e].astype(F32) + one
            run[e] = total

    def block_sum(k, r):
        return run_e[lists[7, k * blocks + r]] + run_l[lists[8, k * blocks + r]]

    waiting = []
    for hop in range(hops):
        def own_block(b, carry):
            agg[b] = jnp.dot(self_ref[b], nodes_e[hop][c * blocks + b], preferred_element_type=F32)
            return carry

        lax.fori_loop(0, blocks, own_block, 0, unroll=2)
        for p in range(parts):
            ref = nodes_e[hop].at[seat(oc, p)]
            arrived(ref, nd_s.at[hop, 0, p], nd_r.at[hop, 0, p], partner)
        if hop == 0:
            ref = adj_e.at[pl.ds(pl.multiple_of(oc * batch, batch), batch)]
            arrived(ref, aj_s.at[0, 0], aj_r.at[0, 0], partner)

        def early(k, carry):
            runs(0, k, hop)
            return carry

        lax.fori_loop(0, kinds, early, 0)
        for p in range(parts):
            ref = nodes_l[hop].at[seat(c, p)]
            arrived(ref, nd_s.at[hop, 1, p], nd_r.at[hop, 1, p], zn)
            go(ref, ref, nd_s.at[hop, 2, p], nd_r.at[hop, 2, p], partner)
        if hop == 0:
            tiles_in(2)
        for p in range(parts):
            ref = nodes_l[hop].at[seat(oc, p)]
            arrived(ref, nd_s.at[hop, 2, p], nd_r.at[hop, 2, p], partner)

        for copy in waiting:
            copy.wait_send()
        waiting = []

        def across(j, k):
            runs(1, k, hop)
            for p in range(parts):
                for r in range(p * per, p * per + per):
                    send1[j, r] = block_sum(k, r).astype(BF)
                piece = pl.ds(p * per, per)
                go(send1.at[j, piece], recv1.at[hop, j, piece], s1.at[hop, j, p], r1.at[hop, j, p], xn, waiting)

        def crossed(j, p):
            ref = recv1.at[hop, j, pl.ds(p * per, per)]
            arrived(ref, s1.at[hop, j, p], r1.at[hop, j, p], xn)

        for j in range(1, far):
            across(j, 2 * j)
        for j in range(1, far):
            runs(1, 2 * j + 1, hop)
            for r in range(blocks):
                mine[j - 1, r] = block_sum(2 * j + 1, r)
        if hop == 0:
            tiles_in(0)
        across(0, 0)
        for p in range(parts):
            piece = pl.ds(p * per, per)
            for j in range(1, far):
                crossed(j, p)
                send2[j - 1, piece] = (mine[j - 1, piece] + recv1[hop, j, piece].astype(F32)).astype(BF)
                go(send2.at[j - 1, piece], recv2.at[hop, j - 1, piece], s2.at[hop, j - 1, p], r2.at[hop, j - 1, p], zdev(j), waiting)
        if hop == 0:
            tiles_in(1)
        runs(1, 1, hop)
        for r in range(blocks):
            agg[r] += block_sum(1, r)
        for p in range(parts):
            piece = pl.ds(p * per, per)
            strip = pl.ds(p * tall, tall)
            crossed(0, p)
            total = agg[piece] + recv1[hop, 0, piece].astype(F32)
            for j in range(1, far):
                arrived(recv2.at[hop, j - 1, piece], s2.at[hop, j - 1, p], r2.at[hop, j - 1, p], zdev(j))
                total += recv2[hop, j - 1, piece].astype(F32)
            gathered = total.astype(BF).reshape(tall, width)
            inner = jnp.dot(gathered, up_ref[hop], preferred_element_type=F32)
            inner = jnp.maximum(inner, 0.0).astype(BF)
            after = state[strip, :] + jnp.dot(inner, down_ref[hop], preferred_element_type=F32)
            if hop == hops - 1:
                out_ref[strip, :] = after.astype(BF)
            else:
                state[strip, :] = after
                nodes_out(hop + 1, p, after)
    for copy in started + waiting:
        copy.wait_send()


def fused(rows, w_proj, w_fc, w_up, w_down, self_adj, adjacency, named, counts, cap):
    tiles = lax.axis_size("tile")
    zs = tiles // CORES
    far = zs // 2
    blocks, slots, tb, _ = adjacency.shape
    width = w_fc.shape[1]
    hops = w_up.shape[0]
    parts = PARTS if blocks % PARTS == 0 else 1
    kinds = 2 * far
    batch = kinds * cap
    span = 2 * cap
    distant = max(1, far - 1)
    vmem = pl.BlockSpec(memory_space=pltpu.VMEM)
    hbm = pl.BlockSpec(memory_space=pltpu.HBM)
    dma = pltpu.SemaphoreType.DMA
    tile = (tb, tb)
    piece = (blocks, tb, width)
    held = (counts, named, rows, w_proj, w_fc, adjacency.reshape((blocks * slots,) + tile), self_adj, w_up, w_down)
    return pl.pallas_call(
        functools.partial(whole_kernel, tiles, cap, parts, hops),
        out_shape=jax.ShapeDtypeStruct((rows.shape[0], width), BF),
        in_specs=[hbm] * 9,
        out_specs=vmem,
        scratch_shapes=[
            pltpu.VMEM(rows.shape, BF),
            pltpu.VMEM(w_fc.shape, BF),
            pltpu.VMEM((rows.shape[1], w_proj.shape[1]), BF),
            pltpu.VMEM((rows.shape[0], w_proj.shape[1]), F32),
            pltpu.VMEM((blocks * slots + 1,) + tile, BF),
            pltpu.VMEM(self_adj.shape, BF),
            pltpu.VMEM(w_up.shape, BF),
            pltpu.VMEM(w_down.shape, BF),
            pltpu.VMEM((16, LANES), jnp.int32),
            pltpu.SMEM((16, LANES), jnp.int32),
            pltpu.VMEM(named.shape, jnp.int32),
            pltpu.SMEM(counts.shape, jnp.int32),
            pltpu.VMEM((3 * batch,) + tile, BF),
            pltpu.VMEM((2 * batch,) + tile, BF),
            pltpu.VMEM((2 * cap,) + tile, BF),
            pltpu.VMEM((2 * cap,) + tile, BF),
            pltpu.VMEM((2 * batch - 4 * cap,) + tile, BF),
            pltpu.VMEM((kinds * span + 1, tb, width), F32),
            pltpu.VMEM((kinds * span + 1, tb, width), F32),
            pltpu.VMEM((rows.shape[0], width), F32),
            pltpu.VMEM(piece, F32),
            pltpu.VMEM((distant,) + piece, F32),
            pltpu.VMEM((far,) + piece, BF),
            pltpu.VMEM((distant,) + piece, BF),
        ]
        + [pltpu.VMEM((2 * blocks, tb, width), BF)] * (2 * hops)
        + [pltpu.VMEM((hops, far) + piece, BF), pltpu.VMEM((hops, distant) + piece, BF)]
        + [dma((10,))]
        + [dma((zs, 2))] * 2
        + [dma((2, zs, 2))] * 2
        + [dma((zs, 2))] * 2
        + [dma((4, zs, 2))] * 2
        + [dma((3, 3))] * 2
        + [dma((hops, 3, parts))] * 2
        + [dma((hops, far, parts))] * 2
        + [dma((hops, distant, parts))] * 2,
        compiler_params=pltpu.CompilerParams(
            collective_id=0, has_side_effects=True, vmem_limit_bytes=48 << 20
        ),
        name="whole",
    )(*(pltpu.with_memory_space_constraint(a, pltpu.HBM) for a in held))


def local(features, w_proj, w_fc, w_up, w_down, self_adj, adjacency, nbr_block, counts):
    rows = features[0]
    blocks = self_adj.shape[1]
    tb = self_adj.shape[2]
    width = w_fc.shape[1]
    slots = adjacency.shape[2]
    hops = w_up.shape[0]
    peers = lax.axis_size("section") * lax.axis_size("tile")
    me_index = lax.axis_index("section") * lax.axis_size("tile") + lax.axis_index("tile")
    sends = blocks * slots
    cap = (sends + peers - 1) // peers
    live = jnp.arange(slots, dtype=jnp.int32)[None, :] < counts[0][:, None]
    square = lax.axis_size("section") == 2 and lax.axis_size("slide") == 2
    pairs = lax.axis_size("tile") % (2 * CORES) == 0
    lanes = nbr_block.shape[1] == LANES and 2 * sends == LANES
    if square and pairs and lanes and sends == peers * cap and w_proj.shape[0] % 32 == 0:
        return fused(rows, w_proj, w_fc, w_up, w_down, self_adj[0], adjacency[0], nbr_block[0].T, counts[0], cap)[None]
    pre = jnp.dot(
        rows,
        lax.all_gather(w_proj, ("section", "tile", "slide"), axis=0, tiled=True),
        preferred_element_type=F32,
    )
    encoded = jax.nn.relu(pre).astype(BF)
    state = jnp.dot(encoded, w_fc, preferred_element_type=F32)
    table = nbr_block[0].reshape(peers, sends)
    target_dev = table // blocks
    target_local = table % blocks
    positions = jnp.arange(sends, dtype=jnp.int32)
    before = positions[None, :] < positions[:, None]
    same = target_dev[:, :, None] == target_dev[:, None, :]
    ranking = jnp.sum(jnp.logical_and(same, before[None]).astype(jnp.int32), axis=2)
    mine_dev = lax.dynamic_index_in_dim(target_dev, me_index, 0, keepdims=False)
    mine_rank = lax.dynamic_index_in_dim(ranking, me_index, 0, keepdims=False)
    slot_of = mine_dev * cap + mine_rank
    send_map = (jnp.arange(peers * cap, dtype=jnp.int32)[:, None] == slot_of[None, :]).astype(BF)
    arrive_hit = target_dev == me_index
    slot_flags = jnp.logical_and(
        arrive_hit[:, :, None],
        ranking[:, :, None] == jnp.arange(cap, dtype=jnp.int32)[None, None, :],
    ).astype(F32)
    local_flags = (
        target_local[:, :, None] == jnp.arange(blocks, dtype=jnp.int32)[None, None, :]
    ).astype(F32)
    recv_map = (
        jnp.einsum("pjc,pjr->rpc", slot_flags, local_flags).reshape(blocks, peers * cap).astype(BF)
    )
    for hop in range(hops):
        nodes = state.astype(BF).reshape(blocks, tb, width)
        own = jnp.einsum("bij,bjh->bih", self_adj[0], nodes, preferred_element_type=F32)
        terms = jnp.einsum("bkij,bjh->bkih", adjacency[0], nodes, preferred_element_type=F32)
        terms = (
            jnp.where(live[:, :, None, None], terms, 0.0).astype(BF).reshape(sends, tb * width)
        )
        outgoing = jnp.dot(send_map, terms, preferred_element_type=F32).astype(BF)
        outgoing = outgoing.reshape(peers, cap, tb, width)
        arrived = lax.all_to_all(
            outgoing, ("section", "tile"), split_axis=0, concat_axis=0, tiled=True
        )
        arrived = arrived.reshape(peers * cap, tb * width)
        incoming = jnp.dot(recv_map, arrived, preferred_element_type=F32).reshape(
            blocks, tb, width
        )
        gathered = (own + incoming).astype(BF).reshape(blocks * tb, width)
        inner = jax.nn.relu(jnp.dot(gathered, w_up[hop], preferred_element_type=F32)).astype(BF)
        state = state + jnp.dot(inner, w_down[hop], preferred_element_type=F32)
    return state.astype(BF)[None]


def solution(mesh):
    return jax.shard_map(
        local,
        mesh=mesh,
        in_specs=(
            P("slide", ("section", "tile"), None),
            P(("section", "tile", "slide"), None),
            P(),
            P(),
            P(),
            P("slide", ("section", "tile"), None, None),
            P("slide", ("section", "tile"), None, None, None),
            P("slide", None, None),
            P("slide", ("section", "tile")),
        ),
        out_specs=P("slide", ("section", "tile"), None),
        check_vma=False,
    )
```

```python
import functools

import jax
import jax.numpy as jnp
from jax import lax
from jax.experimental import pallas as pl
from jax.experimental.pallas import tpu as pltpu
from jax.sharding import PartitionSpec as P

MESH = pl.DeviceIdType.MESH
CORES = 2
LANES = 128
SPLIT = True
WINDOW = 4
NODE_SHARES = (2, 2, 2, 1, 1)
SUM_SHARES = (1, 1, 1, 1, 1, 1, 1, 1)
CUTS = 2
BF = jnp.bfloat16
F32 = jnp.float32


def remote(src, dst, send_sem, recv_sem, device):
    return pltpu.make_async_remote_copy(
        src_ref=src,
        dst_ref=dst,
        send_sem=send_sem,
        recv_sem=recv_sem,
        device_id=device,
        device_id_type=MESH,
    )


def greet(devices):
    barrier = pltpu.get_barrier_semaphore()
    for device in devices:
        pl.semaphore_signal(barrier, inc=1, device_id=device, device_id_type=MESH)
    return lambda: pl.semaphore_wait(barrier, len(devices))


def make_lists(named_ref, counts_ref, table, chips, sizes, place):
    tiles, cap, blocks, far = sizes
    sx, z, oz, c = place
    zs = tiles // CORES
    kinds = 2 * far
    span = 2 * cap
    both = CORES * blocks
    slots = named_ref.shape[0]
    sends = blocks * slots

    def iota(shape, axis):
        return lax.broadcasted_iota(jnp.int32, shape, axis)

    def receiver(kind, gz, gc):
        gx = jnp.where(kind % 2 == 0, 1 - sx, sx)
        return gx * tiles + (gz + 2 * (kind // 2)) % zs * CORES + gc

    lane = iota((1, LANES), 1)
    wide = (LANES, LANES)
    entry = iota(wide, 0)
    column = iota(wide, 1)
    same_core = (entry // blocks) % CORES == (column // blocks) % CORES
    limit = jnp.zeros((1, LANES), jnp.int32)
    for b in range(blocks):
        limit = jnp.where(lane % blocks == b, counts_ref[b], limit)
    alive = (lane // both < limit) & ((lane // blocks) % CORES == c)
    alive = jnp.where(alive, (lane % blocks) * slots + lane // both - sends, 0)
    alive = jnp.transpose(jnp.broadcast_to(alive, wide))
    for phase in range(2):
        row = jnp.zeros((1, LANES), jnp.int32)
        for slot in range(slots):
            moved = pltpu.roll(named_ref[pl.ds(slot, 1), :], (slot * both - chips[phase] * both + LANES) % LANES, 1)
            row = jnp.where(lane // both == slot, moved, row)
        across = jnp.broadcast_to(row * LANES + lane, wide)
        down = jnp.transpose(across)
        named = down // LANES
        less = across < down
        order = jnp.sum(jnp.where(less, 1, 0), axis=1, keepdims=True)
        rank = jnp.sum(jnp.where(less & same_core, 1, 0), axis=1, keepdims=True)
        if phase == 0:
            person = column // (kinds * cap)
            kind = (column // cap) % kinds
            core = jnp.where(person % 2 == 0, c, 1 - c)
            want = receiver(kind, jnp.where(person < 2, z, oz), core) * cap + column % cap
            packed = jnp.sum(jnp.where(rank == want, alive, 0), axis=0, keepdims=True)
            table[pl.ds(0, 1), :] = packed + sends
        kind = column // span % kinds
        want = receiver(kind, z, c) * span + column % span
        hit = order == want
        core = (entry // blocks) % CORES
        rank = jnp.clip(rank - named // blocks * cap, 0, cap - 1)
        if phase == 0:
            tile = core * (kinds * cap) + kind * cap + rank
        else:
            tile = jnp.where(kind < 2, core, core * (kinds - 2) + kind - 2) * cap + rank

        def chosen(value):
            return jnp.sum(jnp.where(hit, value, 0), axis=0, keepdims=True)

        block = chosen(named % blocks)
        table[pl.ds(1 + phase, 1), :] = chosen(tile)
        table[pl.ds(3 + phase, 1), :] = chosen(entry % both)
        again = (lane % span > 0) & (block == pltpu.roll(block, 1, 1))
        table[pl.ds(5 + phase, 1), :] = jnp.where(again, 1, 0)
        block = jnp.transpose(jnp.broadcast_to(block, wide))
        fits = (entry // span == column // blocks) & (entry < kinds * span)
        upto = jnp.sum(jnp.where(fits & (block <= column % blocks), 1, 0), axis=0, keepdims=True)
        there = jnp.sum(jnp.where(fits & (block == column % blocks), 1, 0), axis=0, keepdims=True)
        last = lane // blocks * span + upto - 1
        table[pl.ds(7 + phase, 1), :] = jnp.where(there > 0, last, kinds * span)


def cut(blocks, shares):
    unit = blocks // 8 if blocks % 8 == 0 else 0
    sizes = [unit * share for share in shares] if unit else [blocks]
    return [(sum(sizes[:i]), size) for i, size in enumerate(sizes)]


def node_parts(blocks):
    return cut(blocks, NODE_SHARES)


def sum_parts(blocks):
    return cut(blocks, SUM_SHARES)


def schedule(zs, parts):
    steps = [(m, k) for m in range(zs) for k in range(CUTS)]
    plan = [(1, 1, "lists"), (1, 2, "pack"), (CUTS * (zs // 2) - 1, 1, "tiles"), (5, 5, "ready")]
    for i, (m, k) in enumerate(steps):
        plan += [(i, 0, "line", m, k), (i + 2, 3, "cross", m, k), (i + 4, 4, "corner", m, k)]
        if k < CUTS - 1:
            continue
        for p in range(parts):
            if m < zs - 1 or not SPLIT:
                plan.append((i + 5, 6, "multiply", m, p, (0, 1)))
            else:
                plan.append((i + 4, 6, "multiply", m, p, (0,)))
                plan.append((i + 5, 6, "multiply", m, p, (1,)))
    return [act[2:] for act in sorted(plan, key=lambda act: act[:2])]


def whole_kernel(tiles, cap, hops, counts_hbm, named_hbm, x_hbm, w_hbm, fc_hbm, adj_hbm, self_hbm, up_hbm, down_hbm, out_ref, *scratch):
    scratch = list(scratch)

    def take(count):
        taken = scratch[:count]
        del scratch[:count]
        return taken

    x_ref, fc_ref, w_all, acc, adj_ref, self_ref, up_ref, down_ref = take(8)
    table, lists, named_ref, counts_ref = take(4)
    pack, adj_e, adj_x, adj_n, adj_f, run_e, run_l, state, agg, mine, send1, send2 = take(12)
    nodes_e, nodes_l = take(hops), take(hops)
    recv1, recv2 = take(2)
    ld, z_s, z_r, xy_s, xy_r, dg_s, dg_r, pt_s, pt_r = take(9)
    aj_s, aj_r, nd_s, nd_r, s1, r1, s2, r2 = take(8)

    zs = tiles // CORES
    far = zs // 2
    rows = w_hbm.shape[0]
    half = rows // CUTS
    blocks, tb, width = self_ref.shape[0], self_ref.shape[1], fc_ref.shape[1]
    sends = adj_ref.shape[0] - 1
    kinds = 2 * far
    batch = kinds * cap
    span = 2 * cap
    outs, sums = node_parts(blocks), sum_parts(blocks)
    sx = lax.axis_index("section")
    sy = lax.axis_index("slide")
    t = lax.axis_index("tile")
    z, c = t // CORES, t % CORES
    ox, oy, oc = 1 - sx, 1 - sy, 1 - c
    oz = z + 1 - 2 * (z % 2)
    partner = {"tile": z * CORES + oc}
    xn, yn = {"section": ox}, {"slide": oy}
    zn, zp = {"tile": oz * CORES + c}, {"tile": oz * CORES + oc}
    places = [z] + [(z + 2 * j) % zs for j in range(1, far)] + [oz] + [(oz + 2 * j) % zs for j in range(1, far)]

    def zdev(j):
        return {"tile": ((z + 2 * j) % zs) * CORES + c}

    started = []

    def go(src, dst, ss, rs, device, log=started):
        copy = remote(src, dst, ss, rs, device)
        copy.start()
        log.append(copy)

    def arrived(dst, ss, rs, device):
        remote(dst, dst, ss, rs, device).wait_recv()

    start = ((sx * tiles + t) * 2 + sy) * rows
    loads = [
        pltpu.make_async_copy(src, dst, ld.at[i])
        for i, (src, dst) in enumerate(
            (
                (w_hbm, w_all.at[pl.ds(pl.multiple_of(start, rows), rows)]),
                (adj_hbm, adj_ref.at[pl.ds(0, sends)]),
                (x_hbm, x_ref),
                (fc_hbm, fc_ref),
                (self_hbm, self_ref),
                (up_hbm, up_ref),
                (down_hbm, down_ref),
                (named_hbm, named_ref),
                (counts_hbm, counts_ref),
            )
        )
    ]
    wait = greet([partner, xn, yn, zn, zp] + [zdev(j) for j in range(1, far)])
    for load in loads:
        load.start()
    adj_ref[sends] = jnp.zeros((tb, tb), BF)
    run_e[kinds * span] = jnp.zeros((tb, width), F32)
    run_l[kinds * span] = jnp.zeros((tb, width), F32)

    loads[0].wait()
    wait()

    def at(x, m, core, y, k):
        first = ((x * tiles + places[m] * CORES + core) * 2 + y) * rows + k * half
        return w_all.at[pl.ds(pl.multiple_of(first, half), half)]

    mine_at = [at(sx, 0, c, sy, k) for k in range(CUTS)]
    for k in range(CUTS):
        for j in range(1, far):
            go(mine_at[k], mine_at[k], z_s.at[j, k], z_r.at[j, k], zdev(j))
    for k in range(CUTS):
        go(mine_at[k], mine_at[k], z_s.at[far, k], z_r.at[far, k], zn)

    def line(m, k):
        here = at(sx, m, c, sy, k)
        if 0 < m < far:
            arrived(here, z_s.at[0, k], z_r.at[far - m, k], zdev(m))
        elif m:
            arrived(here, z_s.at[0, k], z_r.at[m, k], zn)
        go(here, here, xy_s.at[0, m, k], xy_r.at[0, m, k], xn)
        go(here, here, xy_s.at[1, m, k], xy_r.at[1, m, k], yn)
        if 0 < m < far:
            go(here, here, z_s.at[far + m, k], z_r.at[far + m, k], zn)
        go(here, here, pt_s.at[0, m, k], pt_r.at[0, m, k], partner)

    def cross(m, k):
        for kind, device, other, ref in (
            (0, xn, yn, at(ox, m, c, sy, k)),
            (1, yn, xn, at(sx, m, c, oy, k)),
        ):
            arrived(ref, xy_s.at[kind, m, k], xy_r.at[kind, m, k], device)
            if k % 2 == kind:
                go(ref, ref, dg_s.at[m, k], dg_r.at[m, k], other)
            go(ref, ref, pt_s.at[1 + kind, m, k], pt_r.at[1 + kind, m, k], partner)

    def corner(m, k):
        ref = at(ox, m, c, oy, k)
        arrived(ref, dg_s.at[m, k], dg_r.at[m, k], (yn, xn)[k % 2])
        go(ref, ref, pt_s.at[3, m, k], pt_r.at[3, m, k], partner)

    def pack_tiles():
        def keep(i, carry):
            adj_e[c * batch + i] = adj_ref[lists[0, i]]
            return carry

        def other(i, carry):
            pack[i] = adj_ref[lists[0, batch + i]]
            return carry

        lax.fori_loop(0, batch, keep, 0, unroll=4)
        lax.fori_loop(0, 3 * batch, other, 0, unroll=4)
        theirs = adj_e.at[pl.ds(pl.multiple_of(c * batch, batch), batch)]
        go(pack.at[pl.ds(0, batch)], theirs, aj_s.at[0, 0], aj_r.at[0, 0], partner)

    near = 2 * cap
    stretch = ((adj_x, 0, cap), (adj_n, cap, cap), (adj_f, near, batch - near))

    def send_tiles(piece):
        into, first, size = stretch[piece]
        for m, device in ((1, zn), (2, zp)):
            there = into.at[pl.ds(pl.multiple_of(c * size, size), size)]
            go(pack.at[pl.ds(m * batch + first, size)], there, aj_s.at[m, piece], aj_r.at[m, piece], device)

    def tiles_in(piece):
        into, first, size = stretch[piece]
        for m, device, core in ((1, zn, c), (2, zp, oc)):
            ref = into.at[pl.ds(pl.multiple_of(core * size, size), size)]
            arrived(ref, aj_s.at[m, piece], aj_r.at[m, piece], device)

    def seat(core, p):
        return pl.ds(core * blocks + outs[p][0], outs[p][1])

    def strip_of(p):
        return pl.ds(outs[p][0] * tb, outs[p][1] * tb)

    def nodes_out(hop, p, after):
        here = nodes_e[hop].at[seat(c, p)]
        here[...] = after.astype(BF).reshape(outs[p][1], tb, width)
        go(here, here, nd_s.at[hop, 0, p], nd_r.at[hop, 0, p], partner)
        go(here, nodes_l[hop].at[seat(c, p)], nd_s.at[hop, 1, p], nd_r.at[hop, 1, p], zn)
        if p == len(outs) - 1:
            go(here, nodes_l[hop].at[seat(c, p)], nd_s.at[hop, 2, p], nd_r.at[hop, 2, p], zp)

    depth = CORES * 2 * rows

    def multiply(m, p, sides):
        if p == 0:
            for k in range(CUTS):
                for kind, (x, y, side) in enumerate(((sx, sy, 0), (ox, sy, 1), (sx, oy, 0), (ox, oy, 1))):
                    if side not in sides:
                        continue
                    arrived(at(x, m, oc, y, k), pt_s.at[kind, m, k], pt_r.at[kind, m, k], partner)
        strip = strip_of(p)
        total = acc[strip, :] if m or 0 not in sides else None
        for side in sides:
            slab = pl.ds(pl.multiple_of(((sx, ox)[side] * zs + places[m]) * depth, depth), depth)
            one = jnp.dot(x_ref[strip, slab], w_all[slab, :], preferred_element_type=F32)
            total = one if total is None else total + one
        if m < zs - 1 or 1 not in sides:
            acc[strip, :] = total
            return
        enc = jnp.maximum(total, 0.0).astype(BF)
        first = jnp.dot(enc, fc_ref[...], preferred_element_type=F32)
        state[strip, :] = first
        nodes_out(0, p, first)
        if p == len(outs) - 1:
            send_tiles(1)

    spread = pltpu.make_async_copy(table, lists, ld.at[9])

    def index_lists():
        for load in loads[7:]:
            load.wait()
        make_lists(named_ref, counts_ref, table, [sx * zs + z, sx * zs + oz], (tiles, cap, blocks, far), (sx, z, oz, c))
        spread.start()

    def packing():
        loads[1].wait()
        spread.wait()
        pack_tiles()

    def ready():
        for load in loads[2:7]:
            load.wait()

    def tiles_out():
        send_tiles(2)
        send_tiles(0)

    acts = {"line": line, "cross": cross, "corner": corner, "multiply": multiply, "lists": index_lists, "pack": packing, "tiles": tiles_out, "ready": ready}
    for act, *where in schedule(zs, len(outs)):
        acts[act](*where)

    def runs(phase, k, hop):
        nodes_ref, run = ((nodes_e[hop], run_e), (nodes_l[hop], run_l))[phase]
        tiles_ref = adj_e if phase == 0 else (adj_x, adj_n, adj_f)[min(k, 2)]
        total = None
        for i in range(span):
            e = k * span + i
            tile, node = lists[1 + phase, e], lists[3 + phase, e]
            one = jnp.dot(tiles_ref[tile], nodes_ref[node], preferred_element_type=F32)
            total = one if total is None else total * lists[5 + phase, e].astype(F32) + one
            run[e] = total

    def block_sum(k, r):
        return run_e[lists[7, k * blocks + r]] + run_l[lists[8, k * blocks + r]]

    def forward(hop, p):
        ref = nodes_l[hop].at[seat(c, p)]
        arrived(ref, nd_s.at[hop, 1, p], nd_r.at[hop, 1, p], zn)
        if p < len(outs) - 1:
            go(ref, ref, nd_s.at[hop, 2, p], nd_r.at[hop, 2, p], partner)

    waiting = []
    for hop in range(hops):
        def own_block(b, carry):
            agg[b] = jnp.dot(self_ref[b], nodes_e[hop][c * blocks + b], preferred_element_type=F32)
            return carry

        lax.fori_loop(0, blocks, own_block, 0, unroll=2)
        for p in range(len(outs)):
            ref = nodes_e[hop].at[seat(oc, p)]
            arrived(ref, nd_s.at[hop, 0, p], nd_r.at[hop, 0, p], partner)
        if hop == 0:
            ref = adj_e.at[pl.ds(pl.multiple_of(oc * batch, batch), batch)]
            arrived(ref, aj_s.at[0, 0], aj_r.at[0, 0], partner)

        def early(k, carry):
            runs(0, k, hop)
            return carry

        lax.fori_loop(0, kinds, early, 0)
        for p in range(len(outs)):
            forward(hop, p)
        if hop == 0:
            tiles_in(2)
        for p in range(len(outs)):
            ref = nodes_l[hop].at[seat(oc, p)]
            arrived(ref, nd_s.at[hop, 2, p], nd_r.at[hop, 2, p], partner)

        for copy in waiting:
            copy.wait_send()
        waiting = []

        def across(j, k):
            runs(1, k, hop)
            for p, (first, size) in enumerate(sums):
                for r in range(first, first + size):
                    send1[j, r] = block_sum(k, r).astype(BF)
                piece = pl.ds(first, size)
                go(send1.at[j, piece], recv1.at[hop, j, piece], s1.at[hop, j, p], r1.at[hop, j, p], xn, waiting)

        def crossed(j, p):
            ref = recv1.at[hop, j, pl.ds(*sums[p])]
            arrived(ref, s1.at[hop, j, p], r1.at[hop, j, p], xn)

        for j in range(1, far):
            across(j, 2 * j)
        for j in range(1, far):
            runs(1, 2 * j + 1, hop)
            for r in range(blocks):
                mine[j - 1, r] = block_sum(2 * j + 1, r)
        if hop == 0:
            tiles_in(0)
        across(0, 0)
        def relay(p):
            piece = pl.ds(*sums[p])
            for j in range(1, far):
                crossed(j, p)
                send2[j - 1, piece] = (mine[j - 1, piece] + recv1[hop, j, piece].astype(F32)).astype(BF)
                go(send2.at[j - 1, piece], recv2.at[hop, j - 1, piece], s2.at[hop, j - 1, p], r2.at[hop, j - 1, p], zdev(j), waiting)

        for p in range(min(WINDOW, len(sums))):
            relay(p)
        if hop == 0:
            tiles_in(1)
        runs(1, 1, hop)
        for r in range(blocks):
            agg[r] += block_sum(1, r)
        for p, (first, size) in enumerate(outs):
            piece = pl.ds(first, size)
            strip = strip_of(p)
            for q, (begin, length) in enumerate(sums):
                if not first <= begin < first + size:
                    continue
                crossed(0, q)
                for j in range(1, far):
                    ref = recv2.at[hop, j - 1, pl.ds(begin, length)]
                    arrived(ref, s2.at[hop, j - 1, q], r2.at[hop, j - 1, q], zdev(j))
                if q + WINDOW < len(sums):
                    relay(q + WINDOW)
            total = agg[piece] + recv1[hop, 0, piece].astype(F32)
            for j in range(1, far):
                total += recv2[hop, j - 1, piece].astype(F32)
            gathered = total.astype(BF).reshape(size * tb, width)
            inner = jnp.dot(gathered, up_ref[hop], preferred_element_type=F32)
            inner = jnp.maximum(inner, 0.0).astype(BF)
            after = state[strip, :] + jnp.dot(inner, down_ref[hop], preferred_element_type=F32)
            if hop == hops - 1:
                out_ref[strip, :] = after.astype(BF)
            else:
                state[strip, :] = after
                nodes_out(hop + 1, p, after)
    for copy in started + waiting:
        copy.wait_send()


def fused(rows, w_proj, w_fc, w_up, w_down, self_adj, adjacency, named, counts, cap):
    tiles = lax.axis_size("tile")
    zs = tiles // CORES
    far = zs // 2
    blocks, slots, tb, _ = adjacency.shape
    width = w_fc.shape[1]
    hops = w_up.shape[0]
    parts, pieces = len(node_parts(blocks)), len(sum_parts(blocks))
    kinds = 2 * far
    batch = kinds * cap
    span = 2 * cap
    distant = max(1, far - 1)
    vmem = pl.BlockSpec(memory_space=pltpu.VMEM)
    hbm = pl.BlockSpec(memory_space=pltpu.HBM)
    dma = pltpu.SemaphoreType.DMA
    tile = (tb, tb)
    piece = (blocks, tb, width)
    held = (counts, named, rows, w_proj, w_fc, adjacency.reshape((blocks * slots,) + tile), self_adj, w_up, w_down)
    return pl.pallas_call(
        functools.partial(whole_kernel, tiles, cap, hops),
        out_shape=jax.ShapeDtypeStruct((rows.shape[0], width), BF),
        in_specs=[hbm] * 9,
        out_specs=vmem,
        scratch_shapes=[
            pltpu.VMEM(rows.shape, BF),
            pltpu.VMEM(w_fc.shape, BF),
            pltpu.VMEM((rows.shape[1], w_proj.shape[1]), BF),
            pltpu.VMEM((rows.shape[0], w_proj.shape[1]), F32),
            pltpu.VMEM((blocks * slots + 1,) + tile, BF),
            pltpu.VMEM(self_adj.shape, BF),
            pltpu.VMEM(w_up.shape, BF),
            pltpu.VMEM(w_down.shape, BF),
            pltpu.VMEM((16, LANES), jnp.int32),
            pltpu.SMEM((16, LANES), jnp.int32),
            pltpu.VMEM(named.shape, jnp.int32),
            pltpu.SMEM(counts.shape, jnp.int32),
            pltpu.VMEM((3 * batch,) + tile, BF),
            pltpu.VMEM((2 * batch,) + tile, BF),
            pltpu.VMEM((2 * cap,) + tile, BF),
            pltpu.VMEM((2 * cap,) + tile, BF),
            pltpu.VMEM((2 * batch - 4 * cap,) + tile, BF),
            pltpu.VMEM((kinds * span + 1, tb, width), F32),
            pltpu.VMEM((kinds * span + 1, tb, width), F32),
            pltpu.VMEM((rows.shape[0], width), F32),
            pltpu.VMEM(piece, F32),
            pltpu.VMEM((distant,) + piece, F32),
            pltpu.VMEM((far,) + piece, BF),
            pltpu.VMEM((distant,) + piece, BF),
        ]
        + [pltpu.VMEM((2 * blocks, tb, width), BF)] * (2 * hops)
        + [pltpu.VMEM((hops, far) + piece, BF), pltpu.VMEM((hops, distant) + piece, BF)]
        + [dma((10,))]
        + [dma((zs, CUTS))] * 2
        + [dma((2, zs, CUTS))] * 2
        + [dma((zs, CUTS))] * 2
        + [dma((4, zs, CUTS))] * 2
        + [dma((3, 3))] * 2
        + [dma((hops, 3, parts))] * 2
        + [dma((hops, far, pieces))] * 2
        + [dma((hops, distant, pieces))] * 2,
        compiler_params=pltpu.CompilerParams(
            collective_id=0, has_side_effects=True, vmem_limit_bytes=48 << 20
        ),
        name="whole",
    )(*(pltpu.with_memory_space_constraint(a, pltpu.HBM) for a in held))


def local(features, w_proj, w_fc, w_up, w_down, self_adj, adjacency, nbr_block, counts):
    rows = features[0]
    blocks = self_adj.shape[1]
    tb = self_adj.shape[2]
    width = w_fc.shape[1]
    slots = adjacency.shape[2]
    hops = w_up.shape[0]
    peers = lax.axis_size("section") * lax.axis_size("tile")
    me_index = lax.axis_index("section") * lax.axis_size("tile") + lax.axis_index("tile")
    sends = blocks * slots
    cap = (sends + peers - 1) // peers
    live = jnp.arange(slots, dtype=jnp.int32)[None, :] < counts[0][:, None]
    square = lax.axis_size("section") == 2 and lax.axis_size("slide") == 2
    pairs = lax.axis_size("tile") % (2 * CORES) == 0
    lanes = nbr_block.shape[1] == LANES and 2 * sends == LANES
    if square and pairs and lanes and sends == peers * cap and w_proj.shape[0] % 32 == 0:
        return fused(rows, w_proj, w_fc, w_up, w_down, self_adj[0], adjacency[0], nbr_block[0].T, counts[0], cap)[None]
    pre = jnp.dot(
        rows,
        lax.all_gather(w_proj, ("section", "tile", "slide"), axis=0, tiled=True),
        preferred_element_type=F32,
    )
    encoded = jax.nn.relu(pre).astype(BF)
    state = jnp.dot(encoded, w_fc, preferred_element_type=F32)
    table = nbr_block[0].reshape(peers, sends)
    target_dev = table // blocks
    target_local = table % blocks
    positions = jnp.arange(sends, dtype=jnp.int32)
    before = positions[None, :] < positions[:, None]
    same = target_dev[:, :, None] == target_dev[:, None, :]
    ranking = jnp.sum(jnp.logical_and(same, before[None]).astype(jnp.int32), axis=2)
    mine_dev = lax.dynamic_index_in_dim(target_dev, me_index, 0, keepdims=False)
    mine_rank = lax.dynamic_index_in_dim(ranking, me_index, 0, keepdims=False)
    slot_of = mine_dev * cap + mine_rank
    send_map = (jnp.arange(peers * cap, dtype=jnp.int32)[:, None] == slot_of[None, :]).astype(BF)
    arrive_hit = target_dev == me_index
    slot_flags = jnp.logical_and(
        arrive_hit[:, :, None],
        ranking[:, :, None] == jnp.arange(cap, dtype=jnp.int32)[None, None, :],
    ).astype(F32)
    local_flags = (
        target_local[:, :, None] == jnp.arange(blocks, dtype=jnp.int32)[None, None, :]
    ).astype(F32)
    recv_map = (
        jnp.einsum("pjc,pjr->rpc", slot_flags, local_flags).reshape(blocks, peers * cap).astype(BF)
    )
    for hop in range(hops):
        nodes = state.astype(BF).reshape(blocks, tb, width)
        own = jnp.einsum("bij,bjh->bih", self_adj[0], nodes, preferred_element_type=F32)
        terms = jnp.einsum("bkij,bjh->bkih", adjacency[0], nodes, preferred_element_type=F32)
        terms = (
            jnp.where(live[:, :, None, None], terms, 0.0).astype(BF).reshape(sends, tb * width)
        )
        outgoing = jnp.dot(send_map, terms, preferred_element_type=F32).astype(BF)
        outgoing = outgoing.reshape(peers, cap, tb, width)
        arrived = lax.all_to_all(
            outgoing, ("section", "tile"), split_axis=0, concat_axis=0, tiled=True
        )
        arrived = arrived.reshape(peers * cap, tb * width)
        incoming = jnp.dot(recv_map, arrived, preferred_element_type=F32).reshape(
            blocks, tb, width
        )
        gathered = (own + incoming).astype(BF).reshape(blocks * tb, width)
        inner = jax.nn.relu(jnp.dot(gathered, w_up[hop], preferred_element_type=F32)).astype(BF)
        state = state + jnp.dot(inner, w_down[hop], preferred_element_type=F32)
    return state.astype(BF)[None]


def solution(mesh):
    return jax.shard_map(
        local,
        mesh=mesh,
        in_specs=(
            P("slide", ("section", "tile"), None),
            P(("section", "tile", "slide"), None),
            P(),
            P(),
            P(),
            P("slide", ("section", "tile"), None, None),
            P("slide", ("section", "tile"), None, None, None),
            P("slide", None, None),
            P("slide", ("section", "tile")),
        ),
        out_specs=P("slide", ("section", "tile"), None),
        check_vma=False,
    )
```

```python
import functools

import jax
import jax.numpy as jnp
from jax import lax
from jax.experimental import pallas as pl
from jax.experimental.pallas import tpu as pltpu
from jax.sharding import PartitionSpec as P

MESH = pl.DeviceIdType.MESH
CORES = 2
LANES = 128
SPLIT = True
WINDOW = 4
NODE_SHARES = (2, 2, 2, 1, 1)
SUM_SHARES = (1, 1, 1, 1, 1, 1, 1, 1)
CUTS = 2
BF = jnp.bfloat16
F32 = jnp.float32


def remote(src, dst, send_sem, recv_sem, device):
    return pltpu.make_async_remote_copy(
        src_ref=src,
        dst_ref=dst,
        send_sem=send_sem,
        recv_sem=recv_sem,
        device_id=device,
        device_id_type=MESH,
    )


def greet(devices):
    barrier = pltpu.get_barrier_semaphore()
    for device in devices:
        pl.semaphore_signal(barrier, inc=1, device_id=device, device_id_type=MESH)
    return lambda: pl.semaphore_wait(barrier, len(devices))


def make_lists(named_ref, counts_ref, table, chips, sizes, place):
    tiles, cap, blocks, far = sizes
    sx, z, oz, c = place
    zs = tiles // CORES
    kinds = 2 * far
    span = 2 * cap
    both = CORES * blocks
    slots = named_ref.shape[0]
    sends = blocks * slots

    def iota(shape, axis):
        return lax.broadcasted_iota(jnp.int32, shape, axis)

    def receiver(kind, gz, gc):
        gx = jnp.where(kind % 2 == 0, 1 - sx, sx)
        return gx * tiles + (gz + 2 * (kind // 2)) % zs * CORES + gc

    lane = iota((1, LANES), 1)
    wide = (LANES, LANES)
    entry = iota(wide, 0)
    column = iota(wide, 1)
    same_core = (entry // blocks) % CORES == (column // blocks) % CORES
    limit = jnp.zeros((1, LANES), jnp.int32)
    for b in range(blocks):
        limit = jnp.where(lane % blocks == b, counts_ref[b], limit)
    alive = (lane // both < limit) & ((lane // blocks) % CORES == c)
    alive = jnp.where(alive, (lane % blocks) * slots + lane // both - sends, 0)
    alive = jnp.transpose(jnp.broadcast_to(alive, wide))
    for phase in range(2):
        row = jnp.zeros((1, LANES), jnp.int32)
        for slot in range(slots):
            moved = pltpu.roll(named_ref[pl.ds(slot, 1), :], (slot * both - chips[phase] * both + LANES) % LANES, 1)
            row = jnp.where(lane // both == slot, moved, row)
        across = jnp.broadcast_to(row * LANES + lane, wide)
        down = jnp.transpose(across)
        named = down // LANES
        less = across < down
        order = jnp.sum(jnp.where(less, 1, 0), axis=1, keepdims=True)
        rank = jnp.sum(jnp.where(less & same_core, 1, 0), axis=1, keepdims=True)
        if phase == 0:
            person = column // (kinds * cap)
            kind = (column // cap) % kinds
            core = jnp.where(person % 2 == 0, c, 1 - c)
            want = receiver(kind, jnp.where(person < 2, z, oz), core) * cap + column % cap
            packed = jnp.sum(jnp.where(rank == want, alive, 0), axis=0, keepdims=True)
            table[pl.ds(0, 1), :] = packed + sends
        kind = column // span % kinds
        want = receiver(kind, z, c) * span + column % span
        hit = order == want
        core = (entry // blocks) % CORES
        rank = jnp.clip(rank - named // blocks * cap, 0, cap - 1)
        if phase == 0:
            tile = core * (kinds * cap) + kind * cap + rank
        else:
            tile = jnp.where(kind < 2, core, core * (kinds - 2) + kind - 2) * cap + rank

        def chosen(value):
            return jnp.sum(jnp.where(hit, value, 0), axis=0, keepdims=True)

        block = chosen(named % blocks)
        table[pl.ds(1 + phase, 1), :] = chosen(tile)
        table[pl.ds(3 + phase, 1), :] = chosen(entry % both)
        again = (lane % span > 0) & (block == pltpu.roll(block, 1, 1))
        table[pl.ds(5 + phase, 1), :] = jnp.where(again, 1, 0)
        block = jnp.transpose(jnp.broadcast_to(block, wide))
        fits = (entry // span == column // blocks) & (entry < kinds * span)
        upto = jnp.sum(jnp.where(fits & (block <= column % blocks), 1, 0), axis=0, keepdims=True)
        there = jnp.sum(jnp.where(fits & (block == column % blocks), 1, 0), axis=0, keepdims=True)
        last = lane // blocks * span + upto - 1
        table[pl.ds(7 + phase, 1), :] = jnp.where(there > 0, last, kinds * span)


def cut(blocks, shares):
    unit = blocks // 8 if blocks % 8 == 0 else 0
    sizes = [unit * share for share in shares] if unit else [blocks]
    return [(sum(sizes[:i]), size) for i, size in enumerate(sizes)]


def node_parts(blocks):
    return cut(blocks, NODE_SHARES)


def sum_parts(blocks):
    return cut(blocks, SUM_SHARES)


def schedule(zs, parts):
    steps = [(m, k) for m in range(zs) for k in range(CUTS)]
    plan = [(1, 1, "lists"), (1, 2, "pack"), (CUTS * (zs // 2) - 1, 1, "tiles"), (5, 5, "ready")]
    for i, (m, k) in enumerate(steps):
        plan += [(i, 0, "line", m, k), (i + 2, 3, "cross", m, k), (i + 4, 4, "corner", m, k)]
        if k < CUTS - 1:
            continue
        for p in range(parts):
            if m < zs - 1 or not SPLIT:
                plan.append((i + 5, 6, "multiply", m, p, (0, 1)))
            else:
                plan.append((i + 4, 6, "multiply", m, p, (0,)))
                plan.append((i + 5, 6, "multiply", m, p, (1,)))
    return [act[2:] for act in sorted(plan, key=lambda act: act[:2])]


def whole_kernel(tiles, cap, hops, counts_hbm, named_hbm, x_hbm, w_hbm, fc_hbm, adj_hbm, self_hbm, up_hbm, down_hbm, out_ref, *scratch):
    scratch = list(scratch)

    def take(count):
        taken = scratch[:count]
        del scratch[:count]
        return taken

    x_ref, fc_ref, w_all, acc, adj_ref, self_ref, up_ref, down_ref = take(8)
    table, lists, named_ref, counts_ref = take(4)
    pack, adj_e, adj_x, adj_n, adj_f, run_e, run_l, state, agg, mine, send1, send2 = take(12)
    nodes_e, nodes_l = take(hops), take(hops)
    recv1, recv2 = take(2)
    ld, z_s, z_r, xy_s, xy_r, dg_s, dg_r, pt_s, pt_r = take(9)
    aj_s, aj_r, nd_s, nd_r, s1, r1, s2, r2 = take(8)

    zs = tiles // CORES
    far = zs // 2
    rows = w_hbm.shape[0]
    half = rows // CUTS
    blocks, tb, width = self_ref.shape[0], self_ref.shape[1], fc_ref.shape[1]
    sends = adj_ref.shape[0] - 1
    kinds = 2 * far
    batch = kinds * cap
    span = 2 * cap
    outs, sums = node_parts(blocks), sum_parts(blocks)
    sx = lax.axis_index("section")
    sy = lax.axis_index("slide")
    t = lax.axis_index("tile")
    z, c = t // CORES, t % CORES
    ox, oy, oc = 1 - sx, 1 - sy, 1 - c
    oz = z + 1 - 2 * (z % 2)
    partner = {"tile": z * CORES + oc}
    xn, yn = {"section": ox}, {"slide": oy}
    zn, zp = {"tile": oz * CORES + c}, {"tile": oz * CORES + oc}
    places = [z] + [(z + 2 * j) % zs for j in range(1, far)] + [oz] + [(oz + 2 * j) % zs for j in range(1, far)]

    def zdev(j):
        return {"tile": ((z + 2 * j) % zs) * CORES + c}

    started = []

    def go(src, dst, ss, rs, device, log=started):
        copy = remote(src, dst, ss, rs, device)
        copy.start()
        log.append(copy)

    def arrived(dst, ss, rs, device):
        remote(dst, dst, ss, rs, device).wait_recv()

    start = ((sx * tiles + t) * 2 + sy) * rows
    loads = [
        pltpu.make_async_copy(src, dst, ld.at[i])
        for i, (src, dst) in enumerate(
            (
                (w_hbm, w_all.at[pl.ds(pl.multiple_of(start, rows), rows)]),
                (adj_hbm, adj_ref.at[pl.ds(0, sends)]),
                (x_hbm, x_ref),
                (fc_hbm, fc_ref),
                (self_hbm, self_ref),
                (up_hbm, up_ref),
                (down_hbm, down_ref),
                (named_hbm, named_ref),
                (counts_hbm, counts_ref),
            )
        )
    ]
    wait = greet([partner, xn, yn, zn, zp] + [zdev(j) for j in range(1, far)])
    for load in loads:
        load.start()
    adj_ref[sends] = jnp.zeros((tb, tb), BF)
    run_e[kinds * span] = jnp.zeros((tb, width), F32)
    run_l[kinds * span] = jnp.zeros((tb, width), F32)

    loads[0].wait()
    wait()

    def at(x, m, core, y, k):
        first = ((x * tiles + places[m] * CORES + core) * 2 + y) * rows + k * half
        return w_all.at[pl.ds(pl.multiple_of(first, half), half)]

    mine_at = [at(sx, 0, c, sy, k) for k in range(CUTS)]
    for k in range(CUTS):
        for j in range(1, far):
            go(mine_at[k], mine_at[k], z_s.at[j, k], z_r.at[j, k], zdev(j))
    for k in range(CUTS):
        go(mine_at[k], mine_at[k], z_s.at[far, k], z_r.at[far, k], zn)

    def line(m, k):
        here = at(sx, m, c, sy, k)
        if 0 < m < far:
            arrived(here, z_s.at[0, k], z_r.at[far - m, k], zdev(m))
        elif m:
            arrived(here, z_s.at[0, k], z_r.at[m, k], zn)
        go(here, here, xy_s.at[0, m, k], xy_r.at[0, m, k], xn)
        go(here, here, xy_s.at[1, m, k], xy_r.at[1, m, k], yn)
        if 0 < m < far:
            go(here, here, z_s.at[far + m, k], z_r.at[far + m, k], zn)
        go(here, here, pt_s.at[0, m, k], pt_r.at[0, m, k], partner)

    def cross(m, k):
        for kind, device, other, ref in (
            (0, xn, yn, at(ox, m, c, sy, k)),
            (1, yn, xn, at(sx, m, c, oy, k)),
        ):
            arrived(ref, xy_s.at[kind, m, k], xy_r.at[kind, m, k], device)
            if k % 2 == kind:
                go(ref, ref, dg_s.at[m, k], dg_r.at[m, k], other)
            go(ref, ref, pt_s.at[1 + kind, m, k], pt_r.at[1 + kind, m, k], partner)

    def corner(m, k):
        ref = at(ox, m, c, oy, k)
        arrived(ref, dg_s.at[m, k], dg_r.at[m, k], (yn, xn)[k % 2])
        go(ref, ref, pt_s.at[3, m, k], pt_r.at[3, m, k], partner)

    def pack_tiles():
        def keep(i, carry):
            adj_e[c * batch + i] = adj_ref[lists[0, i]]
            return carry

        def other(i, carry):
            pack[i] = adj_ref[lists[0, batch + i]]
            return carry

        lax.fori_loop(0, batch, keep, 0, unroll=4)
        lax.fori_loop(0, 3 * batch, other, 0, unroll=4)
        theirs = adj_e.at[pl.ds(pl.multiple_of(c * batch, batch), batch)]
        go(pack.at[pl.ds(0, batch)], theirs, aj_s.at[0, 0], aj_r.at[0, 0], partner)

    near = 2 * cap
    stretch = ((adj_x, 0, cap), (adj_n, cap, cap), (adj_f, near, batch - near))

    def send_tiles(piece):
        into, first, size = stretch[piece]
        for m, device in ((1, zn), (2, zp)):
            there = into.at[pl.ds(pl.multiple_of(c * size, size), size)]
            go(pack.at[pl.ds(m * batch + first, size)], there, aj_s.at[m, piece], aj_r.at[m, piece], device)

    def tiles_in(piece):
        into, first, size = stretch[piece]
        for m, device, core in ((1, zn, c), (2, zp, oc)):
            ref = into.at[pl.ds(pl.multiple_of(core * size, size), size)]
            arrived(ref, aj_s.at[m, piece], aj_r.at[m, piece], device)

    def seat(core, p):
        return pl.ds(core * blocks + outs[p][0], outs[p][1])

    def strip_of(p):
        return pl.ds(outs[p][0] * tb, outs[p][1] * tb)

    def nodes_out(hop, p, after):
        here = nodes_e[hop].at[seat(c, p)]
        here[...] = after.astype(BF).reshape(outs[p][1], tb, width)
        go(here, here, nd_s.at[hop, 0, p], nd_r.at[hop, 0, p], partner)
        go(here, nodes_l[hop].at[seat(c, p)], nd_s.at[hop, 1, p], nd_r.at[hop, 1, p], zn)
        if p == len(outs) - 1:
            go(here, nodes_l[hop].at[seat(c, p)], nd_s.at[hop, 2, p], nd_r.at[hop, 2, p], zp)

    depth = CORES * 2 * rows

    def multiply(m, p, sides):
        if p == 0:
            for k in range(CUTS):
                for kind, (x, y, side) in enumerate(((sx, sy, 0), (ox, sy, 1), (sx, oy, 0), (ox, oy, 1))):
                    if side not in sides:
                        continue
                    arrived(at(x, m, oc, y, k), pt_s.at[kind, m, k], pt_r.at[kind, m, k], partner)
        strip = strip_of(p)
        total = acc[strip, :] if m or 0 not in sides else None
        for side in sides:
            slab = pl.ds(pl.multiple_of(((sx, ox)[side] * zs + places[m]) * depth, depth), depth)
            one = jnp.dot(x_ref[strip, slab], w_all[slab, :], preferred_element_type=F32)
            total = one if total is None else total + one
        if m < zs - 1 or 1 not in sides:
            acc[strip, :] = total
            return
        enc = jnp.maximum(total, 0.0).astype(BF)
        first = jnp.dot(enc, fc_ref[...], preferred_element_type=F32)
        state[strip, :] = first
        nodes_out(0, p, first)
        if p == len(outs) - 1:
            send_tiles(1)

    spread = pltpu.make_async_copy(table, lists, ld.at[9])

    def index_lists():
        for load in loads[7:]:
            load.wait()
        make_lists(named_ref, counts_ref, table, [sx * zs + z, sx * zs + oz], (tiles, cap, blocks, far), (sx, z, oz, c))
        spread.start()

    def packing():
        loads[1].wait()
        spread.wait()
        pack_tiles()

    def ready():
        for load in loads[2:7]:
            load.wait()

    def tiles_out():
        send_tiles(2)
        send_tiles(0)

    acts = {"line": line, "cross": cross, "corner": corner, "multiply": multiply, "lists": index_lists, "pack": packing, "tiles": tiles_out, "ready": ready}
    for act, *where in schedule(zs, len(outs)):
        acts[act](*where)

    def runs(phase, k, hop):
        nodes_ref, run = ((nodes_e[hop], run_e), (nodes_l[hop], run_l))[phase]
        tiles_ref = adj_e if phase == 0 else (adj_x, adj_n, adj_f)[min(k, 2)]
        total = None
        for i in range(span):
            e = k * span + i
            tile, node = lists[1 + phase, e], lists[3 + phase, e]
            one = jnp.dot(tiles_ref[tile], nodes_ref[node], preferred_element_type=F32)
            total = one if total is None else total * lists[5 + phase, e].astype(F32) + one
            run[e] = total

    def block_sum(k, r):
        return run_e[lists[7, k * blocks + r]] + run_l[lists[8, k * blocks + r]]

    def forward(hop, p):
        ref = nodes_l[hop].at[seat(c, p)]
        arrived(ref, nd_s.at[hop, 1, p], nd_r.at[hop, 1, p], zn)
        if p < len(outs) - 1:
            go(ref, ref, nd_s.at[hop, 2, p], nd_r.at[hop, 2, p], partner)

    waiting = []
    for hop in range(hops):
        def own_block(b, carry):
            agg[b] = jnp.dot(self_ref[b], nodes_e[hop][c * blocks + b], preferred_element_type=F32)
            return carry

        for p in range(len(outs)):
            ref = nodes_e[hop].at[seat(oc, p)]
            arrived(ref, nd_s.at[hop, 0, p], nd_r.at[hop, 0, p], partner)
        if hop == 0:
            ref = adj_e.at[pl.ds(pl.multiple_of(oc * batch, batch), batch)]
            arrived(ref, aj_s.at[0, 0], aj_r.at[0, 0], partner)

        def early(k, carry):
            runs(0, k, hop)
            return carry

        lax.fori_loop(2, kinds, early, 0)
        for p in range(len(outs)):
            forward(hop, p)
        if hop == 0:
            tiles_in(2)
        for p in range(len(outs)):
            ref = nodes_l[hop].at[seat(oc, p)]
            arrived(ref, nd_s.at[hop, 2, p], nd_r.at[hop, 2, p], partner)

        for copy in waiting:
            copy.wait_send()
        waiting = []

        def across(j, k):
            runs(1, k, hop)
            for p, (first, size) in enumerate(sums):
                for r in range(first, first + size):
                    send1[j, r] = block_sum(k, r).astype(BF)
                piece = pl.ds(first, size)
                go(send1.at[j, piece], recv1.at[hop, j, piece], s1.at[hop, j, p], r1.at[hop, j, p], xn, waiting)

        def crossed(j, p):
            ref = recv1.at[hop, j, pl.ds(*sums[p])]
            arrived(ref, s1.at[hop, j, p], r1.at[hop, j, p], xn)

        for j in range(1, far):
            across(j, 2 * j)
        for j in range(1, far):
            runs(1, 2 * j + 1, hop)
            for r in range(blocks):
                mine[j - 1, r] = block_sum(2 * j + 1, r)
        lax.fori_loop(0, 2, early, 0)
        lax.fori_loop(0, blocks, own_block, 0, unroll=2)
        if hop == 0:
            tiles_in(0)
        across(0, 0)
        def relay(p):
            piece = pl.ds(*sums[p])
            for j in range(1, far):
                crossed(j, p)
                send2[j - 1, piece] = (mine[j - 1, piece] + recv1[hop, j, piece].astype(F32)).astype(BF)
                go(send2.at[j - 1, piece], recv2.at[hop, j - 1, piece], s2.at[hop, j - 1, p], r2.at[hop, j - 1, p], zdev(j), waiting)

        for p in range(min(WINDOW, len(sums))):
            relay(p)
        if hop == 0:
            tiles_in(1)
        runs(1, 1, hop)
        for r in range(blocks):
            agg[r] += block_sum(1, r)
        for p, (first, size) in enumerate(outs):
            piece = pl.ds(first, size)
            strip = strip_of(p)
            for q, (begin, length) in enumerate(sums):
                if not first <= begin < first + size:
                    continue
                crossed(0, q)
                for j in range(1, far):
                    ref = recv2.at[hop, j - 1, pl.ds(begin, length)]
                    arrived(ref, s2.at[hop, j - 1, q], r2.at[hop, j - 1, q], zdev(j))
                if q + WINDOW < len(sums):
                    relay(q + WINDOW)
            total = agg[piece] + recv1[hop, 0, piece].astype(F32)
            for j in range(1, far):
                total += recv2[hop, j - 1, piece].astype(F32)
            gathered = total.astype(BF).reshape(size * tb, width)
            inner = jnp.dot(gathered, up_ref[hop], preferred_element_type=F32)
            inner = jnp.maximum(inner, 0.0).astype(BF)
            after = state[strip, :] + jnp.dot(inner, down_ref[hop], preferred_element_type=F32)
            if hop == hops - 1:
                out_ref[strip, :] = after.astype(BF)
            else:
                state[strip, :] = after
                nodes_out(hop + 1, p, after)
    for copy in started + waiting:
        copy.wait_send()


def fused(rows, w_proj, w_fc, w_up, w_down, self_adj, adjacency, named, counts, cap):
    tiles = lax.axis_size("tile")
    zs = tiles // CORES
    far = zs // 2
    blocks, slots, tb, _ = adjacency.shape
    width = w_fc.shape[1]
    hops = w_up.shape[0]
    parts, pieces = len(node_parts(blocks)), len(sum_parts(blocks))
    kinds = 2 * far
    batch = kinds * cap
    span = 2 * cap
    distant = max(1, far - 1)
    vmem = pl.BlockSpec(memory_space=pltpu.VMEM)
    hbm = pl.BlockSpec(memory_space=pltpu.HBM)
    dma = pltpu.SemaphoreType.DMA
    tile = (tb, tb)
    piece = (blocks, tb, width)
    held = (counts, named, rows, w_proj, w_fc, adjacency.reshape((blocks * slots,) + tile), self_adj, w_up, w_down)
    return pl.pallas_call(
        functools.partial(whole_kernel, tiles, cap, hops),
        out_shape=jax.ShapeDtypeStruct((rows.shape[0], width), BF),
        in_specs=[hbm] * 9,
        out_specs=vmem,
        scratch_shapes=[
            pltpu.VMEM(rows.shape, BF),
            pltpu.VMEM(w_fc.shape, BF),
            pltpu.VMEM((rows.shape[1], w_proj.shape[1]), BF),
            pltpu.VMEM((rows.shape[0], w_proj.shape[1]), F32),
            pltpu.VMEM((blocks * slots + 1,) + tile, BF),
            pltpu.VMEM(self_adj.shape, BF),
            pltpu.VMEM(w_up.shape, BF),
            pltpu.VMEM(w_down.shape, BF),
            pltpu.VMEM((16, LANES), jnp.int32),
            pltpu.SMEM((16, LANES), jnp.int32),
            pltpu.VMEM(named.shape, jnp.int32),
            pltpu.SMEM(counts.shape, jnp.int32),
            pltpu.VMEM((3 * batch,) + tile, BF),
            pltpu.VMEM((2 * batch,) + tile, BF),
            pltpu.VMEM((2 * cap,) + tile, BF),
            pltpu.VMEM((2 * cap,) + tile, BF),
            pltpu.VMEM((2 * batch - 4 * cap,) + tile, BF),
            pltpu.VMEM((kinds * span + 1, tb, width), F32),
            pltpu.VMEM((kinds * span + 1, tb, width), F32),
            pltpu.VMEM((rows.shape[0], width), F32),
            pltpu.VMEM(piece, F32),
            pltpu.VMEM((distant,) + piece, F32),
            pltpu.VMEM((far,) + piece, BF),
            pltpu.VMEM((distant,) + piece, BF),
        ]
        + [pltpu.VMEM((2 * blocks, tb, width), BF)] * (2 * hops)
        + [pltpu.VMEM((hops, far) + piece, BF), pltpu.VMEM((hops, distant) + piece, BF)]
        + [dma((10,))]
        + [dma((zs, CUTS))] * 2
        + [dma((2, zs, CUTS))] * 2
        + [dma((zs, CUTS))] * 2
        + [dma((4, zs, CUTS))] * 2
        + [dma((3, 3))] * 2
        + [dma((hops, 3, parts))] * 2
        + [dma((hops, far, pieces))] * 2
        + [dma((hops, distant, pieces))] * 2,
        compiler_params=pltpu.CompilerParams(
            collective_id=0, has_side_effects=True, vmem_limit_bytes=48 << 20
        ),
        name="whole",
    )(*(pltpu.with_memory_space_constraint(a, pltpu.HBM) for a in held))


def local(features, w_proj, w_fc, w_up, w_down, self_adj, adjacency, nbr_block, counts):
    rows = features[0]
    blocks = self_adj.shape[1]
    tb = self_adj.shape[2]
    width = w_fc.shape[1]
    slots = adjacency.shape[2]
    hops = w_up.shape[0]
    peers = lax.axis_size("section") * lax.axis_size("tile")
    me_index = lax.axis_index("section") * lax.axis_size("tile") + lax.axis_index("tile")
    sends = blocks * slots
    cap = (sends + peers - 1) // peers
    live = jnp.arange(slots, dtype=jnp.int32)[None, :] < counts[0][:, None]
    square = lax.axis_size("section") == 2 and lax.axis_size("slide") == 2
    pairs = lax.axis_size("tile") % (2 * CORES) == 0
    lanes = nbr_block.shape[1] == LANES and 2 * sends == LANES
    if square and pairs and lanes and sends == peers * cap and w_proj.shape[0] % 32 == 0:
        return fused(rows, w_proj, w_fc, w_up, w_down, self_adj[0], adjacency[0], nbr_block[0].T, counts[0], cap)[None]
    pre = jnp.dot(
        rows,
        lax.all_gather(w_proj, ("section", "tile", "slide"), axis=0, tiled=True),
        preferred_element_type=F32,
    )
    encoded = jax.nn.relu(pre).astype(BF)
    state = jnp.dot(encoded, w_fc, preferred_element_type=F32)
    table = nbr_block[0].reshape(peers, sends)
    target_dev = table // blocks
    target_local = table % blocks
    positions = jnp.arange(sends, dtype=jnp.int32)
    before = positions[None, :] < positions[:, None]
    same = target_dev[:, :, None] == target_dev[:, None, :]
    ranking = jnp.sum(jnp.logical_and(same, before[None]).astype(jnp.int32), axis=2)
    mine_dev = lax.dynamic_index_in_dim(target_dev, me_index, 0, keepdims=False)
    mine_rank = lax.dynamic_index_in_dim(ranking, me_index, 0, keepdims=False)
    slot_of = mine_dev * cap + mine_rank
    send_map = (jnp.arange(peers * cap, dtype=jnp.int32)[:, None] == slot_of[None, :]).astype(BF)
    arrive_hit = target_dev == me_index
    slot_flags = jnp.logical_and(
        arrive_hit[:, :, None],
        ranking[:, :, None] == jnp.arange(cap, dtype=jnp.int32)[None, None, :],
    ).astype(F32)
    local_flags = (
        target_local[:, :, None] == jnp.arange(blocks, dtype=jnp.int32)[None, None, :]
    ).astype(F32)
    recv_map = (
        jnp.einsum("pjc,pjr->rpc", slot_flags, local_flags).reshape(blocks, peers * cap).astype(BF)
    )
    for hop in range(hops):
        nodes = state.astype(BF).reshape(blocks, tb, width)
        own = jnp.einsum("bij,bjh->bih", self_adj[0], nodes, preferred_element_type=F32)
        terms = jnp.einsum("bkij,bjh->bkih", adjacency[0], nodes, preferred_element_type=F32)
        terms = (
            jnp.where(live[:, :, None, None], terms, 0.0).astype(BF).reshape(sends, tb * width)
        )
        outgoing = jnp.dot(send_map, terms, preferred_element_type=F32).astype(BF)
        outgoing = outgoing.reshape(peers, cap, tb, width)
        arrived = lax.all_to_all(
            outgoing, ("section", "tile"), split_axis=0, concat_axis=0, tiled=True
        )
        arrived = arrived.reshape(peers * cap, tb * width)
        incoming = jnp.dot(recv_map, arrived, preferred_element_type=F32).reshape(
            blocks, tb, width
        )
        gathered = (own + incoming).astype(BF).reshape(blocks * tb, width)
        inner = jax.nn.relu(jnp.dot(gathered, w_up[hop], preferred_element_type=F32)).astype(BF)
        state = state + jnp.dot(inner, w_down[hop], preferred_element_type=F32)
    return state.astype(BF)[None]


def solution(mesh):
    return jax.shard_map(
        local,
        mesh=mesh,
        in_specs=(
            P("slide", ("section", "tile"), None),
            P(("section", "tile", "slide"), None),
            P(),
            P(),
            P(),
            P("slide", ("section", "tile"), None, None),
            P("slide", ("section", "tile"), None, None, None),
            P("slide", None, None),
            P("slide", ("section", "tile")),
        ),
        out_specs=P("slide", ("section", "tile"), None),
        check_vma=False,
    )
```
